256 devices in a mesh: domain: 64 (over z, y, x_lo), band: 4 (over x_hi, core).
Axes of the slice: x: 4 (x_hi: 2, x_lo: 2; x = x_hi * 2 + x_lo), y: 4, z: 8, core: 2. Of those that a mesh axis runs over, the one named last changes fastest.
Arguments:
- orbitals: float32 [128, 131072], P('band', 'domain'), may hold values from -6 to 6
- potential: float32 [131072], P('domain'), may hold values from -1 to 1.5
- cell_scale: float32 [2048], P('domain'), may hold values from 0.5 to 2
- connectivity: int32 [125, 2048], P(None, 'domain'), may hold values from 0 to 2559, as said below
- boundary: int32 [32768], P('domain'), may hold values from 0 to 2047, as said below
Outputs:
- filtered: float32 [128, 131072], P('band', 'domain')
- intersection: float32 [128, 128], P('band')
- projected: float32 [128, 128], P('band')
The draws below stay inside these ranges and needn't reach their ends.
Inputs may be any that keep to these rules, and one draw needn't show every extreme that they name: `connectivity`: column c lists cell c's nodes in local order 25 c + 5 b + a; a value below 2048 is a node of the cell's own slab, a value 2048 + g is entry g of the next slab's boundary list (the last slab's next is the first); every node of a slab and every such entry is used. `boundary`: each slab's 512 entries are distinct numbers of its own nodes.
All inputs are finite; a program needn't handle non-finite values. Where the reference program divides by a largest or mean magnitude, that divisor is 1e-20 or more.
Results may differ from the reference program's by a relative error of at most 0.0001.
Values sent between devices are 32-bit elements; how exact they have to be, the bound alone decides.
A program may use at most 64 MiB of HBM per device.

```python
import math
import jax
import jax.numpy as jnp
import numpy as np
from jax import lax

STATES = 128
DEG = 4
EX = 2
EY = 16
PLANE = 512
NODES_DEV = 2048
CELLS_DEV = 32
NODES = 131072
CELLS = 2048


def storage_order(key):
    devices_count = CELLS // CELLS_DEV
    device_keys = jax.random.split(jax.random.fold_in(key, 7), devices_count)

    def one_slab(single):
        order = jax.random.permutation(single, NODES_DEV).astype(jnp.int32)
        turned = (order + (NODES_DEV - 1 - order[0])) % NODES_DEV
        second = turned[1]
        swapped = jnp.where(turned == 0, second, jnp.where(turned == second, 0, turned))
        return swapped.astype(jnp.int32)
    return jax.vmap(one_slab)(device_keys).astype(jnp.int32)


def draw_connectivity(key, part):
    storage = storage_order(key)
    local = jnp.arange(125, dtype=jnp.int32)
    node_x = local % 5
    node_y = local // 5 % 5
    node_z = local // 25
    cell_id = jnp.arange(CELLS_DEV, dtype=jnp.int32)
    cell_x = cell_id % EX
    cell_y = cell_id // EX
    column = (4 * cell_x[None, :] + node_x[:, None]) % (4 * EX)
    row_index = (4 * cell_y[None, :] + node_y[:, None]) % (4 * EY)
    in_plane = row_index * (4 * EX) + column
    canonical = node_z[:, None] * PLANE + in_plane
    inside = jnp.minimum(canonical, NODES_DEV - 1)
    stored = storage[:, inside]
    result = jnp.where(node_z[None, :, None] == 4, NODES_DEV + in_plane[None, :, :], stored)
    return jnp.transpose(result, (1, 0, 2)).reshape(125, CELLS).astype(jnp.int32)


def draw_boundary(key, part):
    storage = storage_order(key)
    return storage[:, :PLANE].reshape(-1).astype(jnp.int32)


def steps_of(stream_key, dims, cuts, least, largest):
    loudness, own = 1.0, jax.random.fold_in(stream_key, 6)
    for position, blocks in cuts:
        steps = jnp.exp(jax.random.uniform(jax.random.fold_in(own, position), (blocks,), jnp.float32, least / len(cuts), largest / len(cuts)))
        loudness = loudness * jnp.repeat(steps, dims[position] // blocks).reshape([-1 if axis == position else 1 for axis in range(len(dims))])
    return loudness


def centred(key, extent, scale, limit, shards=(), kind=jnp.bfloat16):
    values = scale * jax.random.normal(key, extent, jnp.float32)
    if shards:
        values = values * steps_of(key, extent, shards, -0.22, 0.18)
    return jnp.clip(values, -limit, limit).astype(kind)


def setup_inputs(seed: int = 0) -> dict:
    key_list = jax.random.split(jax.random.key(seed), 6)
    return {
        "orbitals": centred(key_list[0], (STATES, NODES), 1.0, 6.0, ((0, 4), (1, 64)), jnp.float32),
        "potential": jnp.clip(-1.0 + 2.5 * jax.random.uniform(key_list[1], (NODES,), jnp.float32) ** steps_of(key_list[1], (NODES,), ((0, 64),), -0.2, 0.2), -1.0, 1.5),
        "cell_scale": jnp.clip(jnp.exp(math.log(2.0) - 1.3862944 * jax.random.uniform(key_list[2], (CELLS,), jnp.float32) ** steps_of(key_list[2], (CELLS,), ((0, 64),), -0.2, 0.2)), 0.5, 2.0),
        "connectivity": draw_connectivity(jax.random.fold_in(key_list[5], 71), 0),
        "boundary": draw_boundary(jax.random.fold_in(key_list[5], 71), 0),
    }


CENTRE = 5.0
SPREAD = 4.0

def gauss_rule():
    inner = math.sqrt(5.0 - 2.0 * math.sqrt(10.0 / 7.0)) / 3.0
    outer = math.sqrt(5.0 + 2.0 * math.sqrt(10.0 / 7.0)) / 3.0
    w_inner = (322.0 + 13.0 * math.sqrt(70.0)) / 900.0
    w_outer = (322.0 - 13.0 * math.sqrt(70.0)) / 900.0
    points = np.array([-outer, -inner, 0.0, inner, outer])
    weights = np.array([w_outer, w_inner, 128.0 / 225.0, w_inner, w_outer])
    return (points, weights)

def element_matrix():
    nodes_1d = np.linspace(0.0, 1.0, 5)
    points, weights = gauss_rule()
    points = 0.5 * (points + 1.0)
    weights = 0.5 * weights
    values = np.ones((5, 5))
    slopes = np.zeros((5, 5))
    for i in range(5):
        for j in range(5):
            if j != i:
                values[i] = values[i] * (points - nodes_1d[j]) / (nodes_1d[i] - nodes_1d[j])
                product_term = np.ones(5) / (nodes_1d[i] - nodes_1d[j])
                for m in range(5):
                    if m != i and m != j:
                        product_term = product_term * (points - nodes_1d[m]) / (nodes_1d[i] - nodes_1d[m])
                slopes[i] = slopes[i] + product_term
    mass_1d = values * weights @ values.T
    stiffness = slopes * weights @ slopes.T
    whole = np.kron(np.kron(stiffness, mass_1d), mass_1d) + np.kron(np.kron(mass_1d, stiffness), mass_1d) + np.kron(np.kron(mass_1d, mass_1d), stiffness)
    return whole / np.max(np.sum(np.abs(whole), axis=1))

def reference(orbitals, potential, cell_scale, connectivity, boundary):
    matrix = jnp.asarray(element_matrix(), jnp.float32)
    devices_count = CELLS // CELLS_DEV
    owner_dev = (jnp.arange(CELLS, dtype=jnp.int32) // CELLS_DEV)[None, :]
    next_dev = (owner_dev + 1) % devices_count
    ghost_slot = jnp.clip(connectivity - NODES_DEV, 0, PLANE - 1)
    remote = next_dev * NODES_DEV + boundary[next_dev * PLANE + ghost_slot]
    global_nodes = jnp.where(connectivity < NODES_DEV, owner_dev * NODES_DEV + connectivity, remote).astype(jnp.int32)
    half_scale = 0.5 * cell_scale

    def apply_row(vector):
        gathered = vector[global_nodes]
        products = jnp.dot(matrix, gathered, precision=lax.Precision.HIGHEST) * half_scale[None, :]
        summed = jnp.zeros((NODES,), jnp.float32).at[global_nodes].add(products)
        return summed + potential * vector

    def apply_all(vectors):
        return lax.map(apply_row, vectors)
    previous = orbitals
    current = (apply_all(orbitals) - CENTRE * orbitals) / SPREAD
    for _ in range(DEG - 1):
        following = 2.0 * (apply_all(current) - CENTRE * current) / SPREAD - previous
        previous, current = (current, following)
    applied = apply_all(current)
    intersection = jnp.dot(current, current.T, precision=lax.Precision.HIGHEST) / NODES
    projected = jnp.dot(applied, current.T, precision=lax.Precision.HIGHEST) / NODES
    return (current, intersection, projected)
```

```python
import math

import jax
import jax.numpy as jnp
import numpy as np
from jax import lax
from jax.experimental import pallas as pl
from jax.experimental.pallas import tpu as pltpu
from jax.sharding import PartitionSpec as P

DEG = 4
CENTRE = 5.0
SPREAD = 4.0
MESH = pl.DeviceIdType.MESH
F32 = jnp.float32
BF16 = jnp.bfloat16
F8 = jnp.float8_e4m3fn
PIECES = 4
STEP = 32.0
TOP = 128.0
LOC = 128
CHUNK = 512


def gauss_rule():
    inner = math.sqrt(5.0 - 2.0 * math.sqrt(10.0 / 7.0)) / 3.0
    outer = math.sqrt(5.0 + 2.0 * math.sqrt(10.0 / 7.0)) / 3.0
    w_inner = (322.0 + 13.0 * math.sqrt(70.0)) / 900.0
    w_outer = (322.0 - 13.0 * math.sqrt(70.0)) / 900.0
    points = np.array([-outer, -inner, 0.0, inner, outer])
    weights = np.array([w_outer, w_inner, 128.0 / 225.0, w_inner, w_outer])
    return (points, weights)


def element_matrix():
    nodes_1d = np.linspace(0.0, 1.0, 5)
    points, weights = gauss_rule()
    points = 0.5 * (points + 1.0)
    weights = 0.5 * weights
    values = np.ones((5, 5))
    slopes = np.zeros((5, 5))
    for i in range(5):
        for j in range(5):
            if j != i:
                values[i] = values[i] * (points - nodes_1d[j]) / (nodes_1d[i] - nodes_1d[j])
                product_term = np.ones(5) / (nodes_1d[i] - nodes_1d[j])
                for m in range(5):
                    if m != i and m != j:
                        product_term = (
                            product_term * (points - nodes_1d[m]) / (nodes_1d[i] - nodes_1d[m])
                        )
                slopes[i] = slopes[i] + product_term
    mass_1d = values * weights @ values.T
    stiffness = slopes * weights @ slopes.T
    whole = (
        np.kron(np.kron(stiffness, mass_1d), mass_1d)
        + np.kron(np.kron(mass_1d, stiffness), mass_1d)
        + np.kron(np.kron(mass_1d, mass_1d), stiffness)
    )
    return whole / np.max(np.sum(np.abs(whole), axis=1))


def element_tile():
    matrix = np.zeros((LOC, LOC), np.float32)
    matrix[:125, :125] = element_matrix().T.astype(np.float32)
    high = matrix.astype(jnp.bfloat16)
    low = (matrix - high.astype(np.float32)).astype(jnp.bfloat16)
    row = np.concatenate([high, low], axis=1)
    return np.concatenate([row, row], axis=0)


def dot(a, b):
    return jnp.dot(a, b, preferred_element_type=F32)


def row_max(x):
    return jnp.maximum(jnp.max(jnp.abs(x), axis=1, keepdims=True), 1e-30)


def cut(x, inverse):
    rest = x * inverse
    pieces = []
    for p in range(PIECES):
        piece = rest.astype(F8)
        pieces.append(piece)
        if p < PIECES - 1:
            rest = (rest - piece.astype(F32)) * STEP
    return pieces


def joined(d, scale, states):
    total = d[(PIECES - 1) * states :]
    for p in range(PIECES - 2, -1, -1):
        total = d[p * states : (p + 1) * states] + total * (1.0 / STEP)
    return total * scale


def kernel(
    n_domain, n_band, nodes_total,
    orb, pot, scl, conn, bnd, kk,
    filt_out, inter_out, proj_out,
    gt, gs, gpt, gps, bt, bs, cpad, pack, packp,
    cur, old, ay, pv, pb, pg, pr, pw, wo, xs, r2,
    bsend, grecv, rsend, rrecv,
    fall, lhs, rhs, part, rsrecv, zbuf, tot,
    pk_ss, pk_rs, b_ss, b_rs, r_ss, r_rs, f_ss, f_rs, s1_ss, s1_rs, s2_ss, s2_rs, s3_ss, s3_rs,
):
    states, nodes = orb.shape
    cells = conn.shape[1]
    ghosts = bnd.shape[0] * bnd.shape[1]
    width = cells * LOC
    per = CHUNK // LOC
    me = lax.axis_index("domain")
    mb = lax.axis_index("band")
    nxt = lax.rem(me + 1, n_domain)
    prv = lax.rem(me + n_domain - 1, n_domain)
    near = mb + 1 - 2 * lax.rem(mb, 2)
    far = lax.rem(mb + 2, n_band)
    q = lax.rem(me, 8)
    z = me // 8
    zs = n_domain // 8
    base = z * 8

    barrier = pltpu.get_barrier_semaphore()

    def greet(where):
        pl.semaphore_signal(barrier, inc=1, device_id=where, device_id_type=MESH)

    greet({"domain": nxt})
    greet({"domain": prv})
    greet({"band": near})
    greet({"band": far})
    for r in range(1, 8):
        greet({"domain": base + lax.rem(q + r, 8)})
    for r in range(1, zs):
        greet({"domain": lax.rem(z + r, zs) * 8 + q})
    greeted = 4 + 7 + zs - 1

    def copy(src, dst, ss, rs, where):
        return pltpu.make_async_remote_copy(
            src_ref=src, dst_ref=dst, send_sem=ss, recv_sem=rs, device_id=where, device_id_type=MESH
        )

    cpad[...] = jnp.full(cpad.shape, -1.0, F32)
    cpad[0 : conn.shape[0], 0:cells] = conn[...].astype(F32)
    pack[0:cells, :] = cpad[...].T[0:cells, :]
    eye = lax.broadcasted_iota(jnp.int32, (cells, cells), 0) == lax.broadcasted_iota(
        jnp.int32, (cells, cells), 1
    )
    factors = jnp.sum(jnp.where(eye, scl[...], 0.0), axis=1, keepdims=True) * 0.5
    pack[cells : 2 * cells, :] = jnp.broadcast_to(factors, (cells, LOC))

    down = lax.broadcasted_iota(jnp.int32, (32, LOC), 0).astype(F32)
    across = lax.broadcasted_iota(jnp.int32, (LOC, LOC), 1).astype(F32)

    def one_hot_t(dst, lanes, row, first, count):
        delta = row - down
        for n in range(0, count, 32):
            dst[n : n + 32, lanes] = jnp.where(delta == float(first + n), 1.0, 0.0).astype(F8)

    def one_hot(dst, rows, row, first, count):
        delta = jnp.broadcast_to(row, (LOC, LOC)).T - across
        for n in range(0, count, LOC):
            dst[rows, n : n + LOC] = jnp.where(delta == float(first + n), 1.0, 0.0).astype(F8)

    for g in range(ghosts // LOC):
        row = bnd[g : g + 1, :].astype(F32)
        one_hot_t(bt, slice(g * LOC, (g + 1) * LOC), row, 0, nodes)
        one_hot(bs, slice(g * LOC, (g + 1) * LOC), row, 0, nodes)

    pl.semaphore_wait(barrier, greeted)
    pack_copy = copy(pack, packp, pk_ss, pk_rs, {"domain": nxt})
    pack_copy.start()

    @pl.loop(0, cells)
    def _(c):
        span = pl.ds(pl.multiple_of(c * LOC, LOC), LOC)
        row = pack[pl.ds(c, 1), :]
        one_hot_t(gt, span, row, 0, nodes + ghosts)
        one_hot(gs, span, row, 0, nodes + ghosts)

    pack_copy.wait()

    @pl.loop(0, cells)
    def _(c):
        span = pl.ds(pl.multiple_of(c * LOC, LOC), LOC)
        row = packp[pl.ds(c, 1), :]
        one_hot_t(gpt, span, row, nodes, ghosts)
        one_hot(gps, span, row, nodes, ghosts)

    cur[...] = orb[...]
    old[...] = orb[...]

    def put(dst, at, pieces):
        for p in range(PIECES):
            dst[p * states : (p + 1) * states, at] = pieces[p]

    def cell_products(d, scale, factor_rows, c0):
        u = joined(d, scale, states)
        for i in range(per):
            one = u[:, i * LOC : (i + 1) * LOC]
            high = one.astype(BF16)
            at = slice((c0 + i) * states, (c0 + i + 1) * states)
            xs[at, 0:LOC] = high
            xs[at, LOC : 2 * LOC] = (one - high.astype(F32)).astype(BF16)
        both = dot(xs[c0 * states : (c0 + per) * states, :], kk[...])
        out = []
        for i in range(per):
            at = slice(i * states, (i + 1) * states)
            out.append((both[at, 0:LOC] + both[at, LOC:]) * factor_rows[c0 + i : c0 + i + 1, :])
        return out

    def application(k, gather):
        y = cur[...]
        top = row_max(y)
        scale, inverse = top * (1.0 / TOP), TOP / top
        put(pv, slice(0, nodes), cut(y, inverse))
        d = dot(pv[...], bt[...])
        pb[...] = d.astype(F8)
        bsend[k] = joined(d, scale, states)
        border = copy(bsend.at[k], grecv.at[k], b_ss.at[k], b_rs.at[k], {"domain": prv})
        border.start()
        if gather:
            f_near = copy(cur, fall.at[mb], f_ss.at[0], f_rs.at[0], {"band": near})
            f_far = copy(cur, fall.at[mb], f_ss.at[1], f_rs.at[1], {"band": far})
            f_near.start()
            f_far.start()

        own = pack.at[cells : 2 * cells, :]
        for n in range(0, width, CHUNK):
            d = dot(pv[...], gt[0:nodes, n : n + CHUNK])
            for i, w in enumerate(cell_products(d, scale, own, n // LOC)):
                at = slice(n + i * LOC, n + (i + 1) * LOC)
                wo[:, at] = w
                put(pw, at, cut(w, inverse))
        rsend[k] = joined(dot(pw[...], gs[:, nodes:]), scale, states)
        back = copy(rsend.at[k], rrecv.at[k], r_ss.at[k], r_rs.at[k], {"domain": nxt})
        back.start()

        before = packp.at[cells : 2 * cells, :]
        for n in range(0, width, CHUNK):
            d = dot(pb[...], gpt[:, n : n + CHUNK])
            for i, w in enumerate(cell_products(d, scale, before, n // LOC)):
                put(pw, slice(n + i * LOC, n + (i + 1) * LOC), cut(w, inverse))
        r2[...] = joined(dot(pw[...], gps[...]), scale, states)

        border.wait()
        ghost = grecv[k]
        top_g = row_max(ghost)
        scale_g, inverse_g = top_g * (1.0 / TOP), TOP / top_g
        put(pg, slice(0, ghosts), cut(ghost, inverse_g))
        both = jnp.maximum(top, top_g)
        scale_b, inverse_b = both * (1.0 / TOP), TOP / both
        for n in range(0, width, CHUNK):
            d = dot(pg[...], gt[nodes:, n : n + CHUNK])
            for i, w in enumerate(cell_products(d, scale_g, own, n // LOC)):
                at = slice(n + i * LOC, n + (i + 1) * LOC)
                put(pw, at, cut(wo[:, at] + w, inverse_b))
        for n in range(0, nodes, CHUNK):
            at = slice(n, n + CHUNK)
            ay[:, at] = joined(dot(pw[...], gs[:, at]), scale_b, states)
        if gather:
            f_near.wait()
            f_far.wait()
            f_pass = copy(fall.at[far], fall.at[far], f_ss.at[2], f_rs.at[2], {"band": near})
            f_pass.start()
        back.wait()
        shared = rrecv[k] + r2[...]
        top_r = row_max(shared)
        put(pr, slice(0, ghosts), cut(shared, TOP / top_r))
        for n in range(0, nodes, CHUNK):
            at = slice(n, n + CHUNK)
            ay[:, at] = ay[:, at] + joined(dot(pr[...], bs[:, at]), top_r * (1.0 / TOP), states)
        for t in range(nodes // LOC):
            at = slice(t * LOC, (t + 1) * LOC)
            ay[:, at] = ay[:, at] + pot[t : t + 1, :] * cur[:, at]
        return f_pass if gather else None

    @pl.loop(0, DEG)
    def _(k):
        application(k, False)
        first = (k == 0).astype(F32)
        alpha = (2.0 - first) / SPREAD
        beta = 1.0 - first
        y = cur[...]
        following = alpha * (ay[...] - CENTRE * y) - beta * old[...]
        old[...] = y
        cur[...] = following

    f_pass = application(DEG, True)
    filt_out[...] = cur[...]
    fall[mb] = cur[...]
    for i, value in enumerate((cur, ay)):
        v = value[...]
        high = v.astype(BF16)
        lhs[2 * i * states : (2 * i + 1) * states, :] = high
        lhs[(2 * i + 1) * states : (2 * i + 2) * states, :] = (v - high.astype(F32)).astype(BF16)
    f_pass.wait()
    everyone = n_band * states
    for j in range(n_band):
        v = fall[j]
        high = v.astype(BF16)
        rhs[j * states : (j + 1) * states, :] = high
        rhs[everyone + j * states : everyone + (j + 1) * states, :] = (v - high.astype(F32)).astype(BF16)
    g = lax.dot_general(
        lhs[...], rhs[...], (((1,), (1,)), ((), ())), preferred_element_type=F32
    )
    g = g[:, :everyone] + g[:, everyone:]
    part[0 : states // 8] = (g[0:states] + g[states : 2 * states]).reshape(states // 8, 8, everyone)
    part[states // 8 :] = (g[2 * states : 3 * states] + g[3 * states :]).reshape(
        states // 8, 8, everyone
    )

    sends = []
    for r in range(1, 8):
        peer = lax.rem(q + r, 8)
        c = copy(part.at[peer], rsrecv.at[r], s1_ss.at[r], s1_rs.at[r], {"domain": base + peer})
        c.start()
        sends.append(c)
    for c in sends:
        c.wait()
    total = part[q]
    for r in range(1, 8):
        total = total + rsrecv[r]
    zbuf[z] = total
    sends = []
    for r in range(1, zs):
        peer = lax.rem(z + r, zs)
        c = copy(zbuf.at[z], zbuf.at[z], s2_ss.at[r], s2_rs.at[r], {"domain": peer * 8 + q})
        c.start()
        sends.append(c)
    for c in sends:
        c.wait()
    total = zbuf[0]
    for r in range(1, zs):
        total = total + zbuf[r]
    tot[q] = total * (1.0 / nodes_total)
    sends = []
    for r in range(1, 8):
        peer = lax.rem(q + r, 8)
        c = copy(tot.at[q], tot.at[q], s3_ss.at[r], s3_rs.at[r], {"domain": base + peer})
        c.start()
        sends.append(c)
    for c in sends:
        c.wait()
    inter_out[...] = tot[0 : states // 8].reshape(states, everyone)
    proj_out[...] = tot[states // 8 :].reshape(states, everyone)


def solution(mesh):
    n_domain, n_band = mesh.shape["domain"], mesh.shape["band"]
    tile = element_tile()

    def per_device(orbitals, potential, cell_scale, connectivity, boundary):
        states, nodes = orbitals.shape
        cells = connectivity.shape[1]
        ghosts = boundary.shape[0]
        width = cells * LOC
        rows = PIECES * states
        everyone = n_band * states
        vm = pltpu.VMEM
        dma = pltpu.SemaphoreType.DMA
        body = lambda *refs: kernel(n_domain, n_band, nodes * n_domain, *refs)
        return pl.pallas_call(
            body,
            name="chebyshev_step",
            out_shape=(
                jax.ShapeDtypeStruct((states, nodes), F32),
                jax.ShapeDtypeStruct((states, everyone), F32),
                jax.ShapeDtypeStruct((states, everyone), F32),
            ),
            in_specs=[pl.BlockSpec(memory_space=vm)] * 6,
            out_specs=(pl.BlockSpec(memory_space=vm),) * 3,
            scratch_shapes=[
                vm((nodes + ghosts, width), F8),
                vm((width, nodes + ghosts), F8),
                vm((ghosts, width), F8),
                vm((width, ghosts), F8),
                vm((nodes, ghosts), F8),
                vm((ghosts, nodes), F8),
                vm((LOC, LOC), F32),
                vm((2 * cells, LOC), F32),
                vm((2 * cells, LOC), F32),
                vm((states, nodes), F32),
                vm((states, nodes), F32),
                vm((states, nodes), F32),
                vm((rows, nodes), F8),
                vm((rows, ghosts), F8),
                vm((rows, ghosts), F8),
                vm((rows, ghosts), F8),
                vm((rows, width), F8),
                vm((states, width), F32),
                vm((cells * states, 2 * LOC), BF16),
                vm((states, ghosts), F32),
                vm((DEG + 1, states, ghosts), F32),
                vm((DEG + 1, states, ghosts), F32),
                vm((DEG + 1, states, ghosts), F32),
                vm((DEG + 1, states, ghosts), F32),
                vm((n_band, states, nodes), F32),
                vm((4 * states, nodes), BF16),
                vm((2 * everyone, nodes), BF16),
                vm((8, 8, everyone), F32),
                vm((8, 8, everyone), F32),
                vm((n_domain // 8, 8, everyone), F32),
                vm((8, 8, everyone), F32),
                dma, dma,
                dma((DEG + 1,)), dma((DEG + 1,)), dma((DEG + 1,)), dma((DEG + 1,)),
                dma((3,)), dma((3,)),
                dma((8,)), dma((8,)), dma((n_domain // 8,)), dma((n_domain // 8,)), dma((8,)), dma((8,)),
            ],
            compiler_params=pltpu.CompilerParams(
                collective_id=0, has_side_effects=True, vmem_limit_bytes=60 * 2**20
            ),
        )(
            orbitals,
            potential.reshape(nodes // LOC, LOC),
            cell_scale.reshape(1, cells),
            connectivity,
            boundary.reshape(ghosts // LOC, LOC),
            jnp.asarray(tile),
        )

    in_specs = (P("band", "domain"), P("domain"), P("domain"), P(None, "domain"), P("domain"))
    out_specs = (P("band", "domain"), P("band", None), P("band", None))
    return jax.shard_map(
        per_device, mesh=mesh, in_specs=in_specs, out_specs=out_specs, check_vma=False
    )
```

```python
import math

import jax
import jax.numpy as jnp
import numpy as np
from jax import lax
from jax.experimental import pallas as pl
from jax.experimental.pallas import tpu as pltpu
from jax.sharding import PartitionSpec as P

DEG = 4
CENTRE = 5.0
SPREAD = 4.0
MESH = pl.DeviceIdType.MESH
F32 = jnp.float32
BF16 = jnp.bfloat16
F8 = jnp.float8_e4m3fn
PIECES = 4
STEP = 32.0
TOP = 128.0
LOC = 128
CHUNK = 512


def gauss_rule():
    inner = math.sqrt(5.0 - 2.0 * math.sqrt(10.0 / 7.0)) / 3.0
    outer = math.sqrt(5.0 + 2.0 * math.sqrt(10.0 / 7.0)) / 3.0
    w_inner = (322.0 + 13.0 * math.sqrt(70.0)) / 900.0
    w_outer = (322.0 - 13.0 * math.sqrt(70.0)) / 900.0
    points = np.array([-outer, -inner, 0.0, inner, outer])
    weights = np.array([w_outer, w_inner, 128.0 / 225.0, w_inner, w_outer])
    return (points, weights)


def element_matrix():
    nodes_1d = np.linspace(0.0, 1.0, 5)
    points, weights = gauss_rule()
    points = 0.5 * (points + 1.0)
    weights = 0.5 * weights
    values = np.ones((5, 5))
    slopes = np.zeros((5, 5))
    for i in range(5):
        for j in range(5):
            if j != i:
                values[i] = values[i] * (points - nodes_1d[j]) / (nodes_1d[i] - nodes_1d[j])
                product_term = np.ones(5) / (nodes_1d[i] - nodes_1d[j])
                for m in range(5):
                    if m != i and m != j:
                        product_term = (
                            product_term * (points - nodes_1d[m]) / (nodes_1d[i] - nodes_1d[m])
                        )
                slopes[i] = slopes[i] + product_term
    mass_1d = values * weights @ values.T
    stiffness = slopes * weights @ slopes.T
    whole = (
        np.kron(np.kron(stiffness, mass_1d), mass_1d)
        + np.kron(np.kron(mass_1d, stiffness), mass_1d)
        + np.kron(np.kron(mass_1d, mass_1d), stiffness)
    )
    return whole / np.max(np.sum(np.abs(whole), axis=1))


def element_tile():
    matrix = np.zeros((LOC, LOC), np.float32)
    matrix[:125, :125] = element_matrix().T.astype(np.float32)
    high = matrix.astype(jnp.bfloat16)
    low = (matrix - high.astype(np.float32)).astype(jnp.bfloat16)
    row = np.concatenate([high, low], axis=1)
    return np.concatenate([row, row], axis=0)


def dot(a, b):
    return jnp.dot(a, b, preferred_element_type=F32)


def row_max(x):
    return jnp.maximum(jnp.max(jnp.abs(x), axis=1, keepdims=True), 1e-30)


def cut(x, inverse):
    rest = x * inverse
    pieces = []
    for p in range(PIECES):
        piece = rest.astype(F8)
        pieces.append(piece)
        if p < PIECES - 1:
            rest = (rest - piece.astype(F32)) * STEP
    return pieces


def joined(d, scale, states):
    total = d[(PIECES - 1) * states :]
    for p in range(PIECES - 2, -1, -1):
        total = d[p * states : (p + 1) * states] + total * (1.0 / STEP)
    return total * scale


def kernel(
    n_domain, n_band, nodes_total,
    orb, pot, scl, conn, bnd, kk,
    filt_out, total_out,
    gt, gs, gpt, gps, bt, bs, pack, packp,
    cur, old, ay, pv, pb, pg, pr, pw, pwp, wo, xs, xsp, r2,
    bsend, grecv, rsend, rrecv,
    fall, lhs, rhs, part, rsrecv, zbuf, tot,
    out_s, pk_ss, pk_rs, b_ss, b_rs, r_ss, r_rs, f_ss, f_rs, s1_ss, s1_rs, s2_ss, s2_rs, s3_ss, s3_rs,
):
    states, nodes = orb.shape
    cells = conn.shape[0]
    ghosts = bnd.shape[0] * bnd.shape[1]
    width = cells * LOC
    me = lax.axis_index("domain")
    mb = lax.axis_index("band")
    nxt = lax.rem(me + 1, n_domain)
    prv = lax.rem(me + n_domain - 1, n_domain)
    near = mb + 1 - 2 * lax.rem(mb, 2)
    far = lax.rem(mb + 2, n_band)
    q = lax.rem(me, 8)
    z = me // 8
    zs = n_domain // 8
    base = z * 8

    barrier = pltpu.get_barrier_semaphore()

    def greet(where):
        pl.semaphore_signal(barrier, inc=1, device_id=where, device_id_type=MESH)

    greet({"domain": nxt})
    greet({"domain": prv})
    greet({"band": near})
    greet({"band": far})
    for r in range(1, 8):
        greet({"domain": base + lax.rem(q + r, 8)})
    for r in range(1, zs):
        greet({"domain": lax.rem(z + r, zs) * 8 + q})
    greeted = 4 + 7 + zs - 1

    def copy(src, dst, ss, rs, where):
        return pltpu.make_async_remote_copy(
            src_ref=src, dst_ref=dst, send_sem=ss, recv_sem=rs, device_id=where, device_id_type=MESH
        )

    pack[0:cells, :] = jnp.full((cells, LOC), -1.0, F32)
    pack[0:cells, 0 : conn.shape[1]] = conn[...].astype(F32)
    eye = lax.broadcasted_iota(jnp.int32, (cells, cells), 0) == lax.broadcasted_iota(
        jnp.int32, (cells, cells), 1
    )
    factors = jnp.sum(jnp.where(eye, scl[...], 0.0), axis=1, keepdims=True) * 0.5
    pack[cells : 2 * cells, :] = jnp.broadcast_to(factors, (cells, LOC))

    down = lax.broadcasted_iota(jnp.int32, (LOC, LOC), 0).astype(F32)
    across = lax.broadcasted_iota(jnp.int32, (LOC, LOC), 1).astype(F32)
    nothing = jnp.zeros((LOC, LOC), F8)

    def one_hot(upright, flat, span, row, first, count):
        block = jnp.floor(row * (1.0 / LOC))
        rest = jnp.broadcast_to(row - block * LOC, (LOC, LOC))
        block = jnp.broadcast_to(block, (LOC, LOC))
        hot_u = jnp.where(rest == down, 1.0, 0.0).astype(F8)
        hot_f = jnp.where(rest.T == across, 1.0, 0.0).astype(F8)
        block_u = block.astype(jnp.int32).astype(jnp.int8)
        block_f = block.T.astype(jnp.int32).astype(jnp.int8)
        for t in range(count // LOC):
            at = slice(t * LOC, (t + 1) * LOC)
            now = jnp.int8(first // LOC + t)
            upright[at, span] = jnp.where(block_u == now, hot_u, nothing)
            flat[span, at] = jnp.where(block_f == now, hot_f, nothing)

    def own_matrices(lo, hi):
        @pl.loop(lo, hi, unroll=4)
        def _(c):
            span = pl.ds(pl.multiple_of(c * LOC, LOC), LOC)
            one_hot(gt, gs, span, pack[pl.ds(c, 1), :], 0, nodes + ghosts)

    for g in range(ghosts // LOC):
        one_hot(bt, bs, slice(g * LOC, (g + 1) * LOC), bnd[g : g + 1, :].astype(F32), 0, nodes)
    own_matrices(0, cells // 2)
    pl.semaphore_wait(barrier, greeted)
    pack_copy = copy(pack, packp, pk_ss, pk_rs, {"domain": nxt})
    pack_copy.start()
    own_matrices(cells // 2, cells)

    cur[...] = orb[...]
    old[...] = orb[...]

    def put(dst, at, pieces):
        for p in range(PIECES):
            dst[p * states : (p + 1) * states, at] = pieces[p]

    def gathered(values, upright, rows, scale, dst):
        for n in range(0, width, CHUNK):
            u = joined(dot(values[...], upright[rows, n : n + CHUNK]), scale, states)
            for i in range(CHUNK // LOC):
                one = u[:, i * LOC : (i + 1) * LOC]
                high = one.astype(BF16)
                at = slice((n // LOC + i) * states, (n // LOC + i + 1) * states)
                dst[at, 0:LOC] = high
                dst[at, LOC : 2 * LOC] = (one - high.astype(F32)).astype(BF16)

    def cell_products(src, factor_rows, use):
        for c0 in range(0, cells, 8):
            both = dot(src[c0 * states : (c0 + 8) * states, :], kk[...])
            for i in range(8):
                at = slice(i * states, (i + 1) * states)
                use(
                    slice((c0 + i) * LOC, (c0 + i + 1) * LOC),
                    (both[at, 0:LOC] + both[at, LOC:]) * factor_rows[c0 + i : c0 + i + 1, :],
                )

    own = pack.at[cells : 2 * cells, :]
    before = packp.at[cells : 2 * cells, :]
    f_near = copy(fall.at[mb], fall.at[mb], f_ss.at[0], f_rs.at[0], {"band": near})
    f_far = copy(fall.at[mb], fall.at[mb], f_ss.at[1], f_rs.at[1], {"band": far})
    f_pass = copy(fall.at[far], fall.at[far], f_ss.at[2], f_rs.at[2], {"band": near})
    f_out = pltpu.make_async_copy(fall.at[mb], filt_out, out_s)

    @pl.loop(0, DEG + 1)
    def _(k):
        y = cur[...]
        top = row_max(y)
        scale, inverse = top * (1.0 / TOP), TOP / top
        put(pv, slice(0, nodes), cut(y, inverse))
        d = dot(pv[...], bt[...])
        pb[...] = d.astype(F8)
        bsend[k] = joined(d, scale, states)
        border = copy(bsend.at[k], grecv.at[k], b_ss.at[k], b_rs.at[k], {"domain": prv})
        border.start()

        @pl.when(k == DEG)
        def _():
            fall[mb] = cur[...]
            f_near.start()
            f_far.start()
            f_out.start()

        gathered(pv, gt, slice(0, nodes), scale, xs)

        def keep(at, w):
            wo[:, at] = w
            put(pw, at, cut(w, inverse))

        cell_products(xs, own, keep)
        rsend[k] = joined(dot(pw[...], gs[:, nodes:]), scale, states)
        back = copy(rsend.at[k], rrecv.at[k], r_ss.at[k], r_rs.at[k], {"domain": nxt})
        back.start()

        @pl.when(k == 0)
        def _():
            pack_copy.wait()

            @pl.loop(0, cells, unroll=4)
            def _(c):
                span = pl.ds(pl.multiple_of(c * LOC, LOC), LOC)
                one_hot(gpt, gps, span, packp[pl.ds(c, 1), :], nodes, ghosts)

        gathered(pb, gpt, slice(0, ghosts), scale, xsp)
        cell_products(xsp, before, lambda at, w: put(pwp, at, cut(w, inverse)))
        r2[...] = joined(dot(pwp[...], gps[...]), scale, states)

        border.wait()
        ghost = grecv[k]
        top_g = row_max(ghost)
        scale_g, inverse_g = top_g * (1.0 / TOP), TOP / top_g
        put(pg, slice(0, ghosts), cut(ghost, inverse_g))
        both = jnp.maximum(top, top_g)
        scale_b, inverse_b = both * (1.0 / TOP), TOP / both
        gathered(pg, gt, slice(nodes, nodes + ghosts), scale_g, xs)
        cell_products(xs, own, lambda at, w: put(pw, at, cut(wo[:, at] + w, inverse_b)))
        for n in range(0, nodes, CHUNK):
            at = slice(n, n + CHUNK)
            ay[:, at] = joined(dot(pw[...], gs[:, at]), scale_b, states)

        @pl.when(k == DEG)
        def _():
            f_near.wait()
            f_far.wait()
            f_pass.start()

        back.wait()
        shared = rrecv[k] + r2[...]
        top_r = row_max(shared)
        put(pr, slice(0, ghosts), cut(shared, TOP / top_r))
        first = (k == 0).astype(F32)
        alpha = (2.0 - first) / SPREAD
        beta = 1.0 - first
        for n in range(0, nodes, CHUNK):
            h = joined(dot(pr[...], bs[:, n : n + CHUNK]), top_r * (1.0 / TOP), states)
            for i in range(CHUNK // LOC):
                at = slice(n + i * LOC, n + (i + 1) * LOC)
                t = n // LOC + i
                v = cur[:, at]
                full = ay[:, at] + h[:, i * LOC : (i + 1) * LOC] + pot[t : t + 1, :] * v
                ay[:, at] = full
                cur[:, at] = alpha * (full - CENTRE * v) - beta * old[:, at]
                old[:, at] = v

    f_out.wait()
    for i, value in enumerate((old, ay)):
        v = value[...]
        high = v.astype(BF16)
        lhs[2 * i * states : (2 * i + 1) * states, :] = high
        lhs[(2 * i + 1) * states : (2 * i + 2) * states, :] = (v - high.astype(F32)).astype(BF16)
    f_pass.wait()
    everyone = n_band * states
    for j in range(n_band):
        v = fall[j]
        high = v.astype(BF16)
        rhs[j * states : (j + 1) * states, :] = high
        rhs[everyone + j * states : everyone + (j + 1) * states, :] = (v - high.astype(F32)).astype(BF16)
    g = lax.dot_general(
        lhs[...], rhs[...], (((1,), (1,)), ((), ())), preferred_element_type=F32
    )
    g = g[:, :everyone] + g[:, everyone:]
    part[0 : states // 8] = (g[0:states] + g[states : 2 * states]).reshape(states // 8, 8, everyone)
    part[states // 8 :] = (g[2 * states : 3 * states] + g[3 * states :]).reshape(
        states // 8, 8, everyone
    )

    sends = []
    for r in range(1, 8):
        peer = lax.rem(q + r, 8)
        c = copy(part.at[peer], rsrecv.at[r], s1_ss.at[r], s1_rs.at[r], {"domain": base + peer})
        c.start()
        sends.append(c)
    for c in sends:
        c.wait()
    total = part[q]
    for r in range(1, 8):
        total = total + rsrecv[r]
    zbuf[z] = total
    sends = []
    for r in range(1, zs):
        peer = lax.rem(z + r, zs)
        c = copy(zbuf.at[z], zbuf.at[z], s2_ss.at[r], s2_rs.at[r], {"domain": peer * 8 + q})
        c.start()
        sends.append(c)
    for c in sends:
        c.wait()
    total = zbuf[0]
    for r in range(1, zs):
        total = total + zbuf[r]
    tot[q] = total * (1.0 / nodes_total)
    sends = []
    for r in range(1, 8):
        peer = lax.rem(q + r, 8)
        c = copy(tot.at[q], tot.at[q], s3_ss.at[r], s3_rs.at[r], {"domain": base + peer})
        c.start()
        sends.append(c)
    for c in sends:
        c.wait()
    total_out[...] = tot[...].reshape(2 * states, everyone)


def write_out(filt, total, filt_out, inter_out, proj_out):
    states = filt.shape[0]
    filt_out[...] = filt[...]
    inter_out[...] = total[0:states, :]
    proj_out[...] = total[states:, :]


def solution(mesh):
    n_domain, n_band = mesh.shape["domain"], mesh.shape["band"]
    tile = element_tile()

    def per_device(orbitals, potential, cell_scale, connectivity, boundary):
        states, nodes = orbitals.shape
        cells = connectivity.shape[1]
        ghosts = boundary.shape[0]
        width = cells * LOC
        rows = PIECES * states
        everyone = n_band * states
        vm = pltpu.VMEM
        dma = pltpu.SemaphoreType.DMA
        body = lambda *refs: kernel(n_domain, n_band, nodes * n_domain, *refs)
        filtered, totals = pl.pallas_call(
            body,
            name="chebyshev_step",
            out_shape=(
                jax.ShapeDtypeStruct((states, nodes), F32),
                jax.ShapeDtypeStruct((2 * states, everyone), F32),
            ),
            in_specs=[pl.BlockSpec(memory_space=vm)] * 6,
            out_specs=(pl.BlockSpec(memory_space=pl.ANY), pl.BlockSpec(memory_space=vm)),
            scratch_shapes=[
                vm((nodes + ghosts, width), F8),
                vm((width, nodes + ghosts), F8),
                vm((ghosts, width), F8),
                vm((width, ghosts), F8),
                vm((nodes, ghosts), F8),
                vm((ghosts, nodes), F8),
                vm((2 * cells, LOC), F32),
                vm((2 * cells, LOC), F32),
                vm((states, nodes), F32),
                vm((states, nodes), F32),
                vm((states, nodes), F32),
                vm((rows, nodes), F8),
                vm((rows, ghosts), F8),
                vm((rows, ghosts), F8),
                vm((rows, ghosts), F8),
                vm((rows, width), F8),
                vm((rows, width), F8),
                vm((states, width), F32),
                vm((cells * states, 2 * LOC), BF16),
                vm((cells * states, 2 * LOC), BF16),
                vm((states, ghosts), F32),
                vm((DEG + 1, states, ghosts), F32),
                vm((DEG + 1, states, ghosts), F32),
                vm((DEG + 1, states, ghosts), F32),
                vm((DEG + 1, states, ghosts), F32),
                vm((n_band, states, nodes), F32),
                vm((4 * states, nodes), BF16),
                vm((2 * everyone, nodes), BF16),
                vm((8, 8, everyone), F32),
                vm((8, 8, everyone), F32),
                vm((n_domain // 8, 8, everyone), F32),
                vm((8, 8, everyone), F32),
                dma, dma, dma,
                dma((DEG + 1,)), dma((DEG + 1,)), dma((DEG + 1,)), dma((DEG + 1,)),
                dma((3,)), dma((3,)),
                dma((8,)), dma((8,)), dma((n_domain // 8,)), dma((n_domain // 8,)), dma((8,)), dma((8,)),
            ],
            compiler_params=pltpu.CompilerParams(
                collective_id=0, has_side_effects=True, vmem_limit_bytes=60 * 2**20
            ),
        )(
            orbitals,
            potential.reshape(nodes // LOC, LOC),
            cell_scale.reshape(1, cells),
            connectivity.T,
            boundary.reshape(ghosts // LOC, LOC),
            jnp.asarray(tile),
        )
        return pl.pallas_call(
            write_out,
            name="outputs",
            out_shape=(
                jax.ShapeDtypeStruct((states, nodes), F32),
                jax.ShapeDtypeStruct((states, everyone), F32),
                jax.ShapeDtypeStruct((states, everyone), F32),
            ),
            in_specs=[pl.BlockSpec(memory_space=vm)] * 2,
            out_specs=(pl.BlockSpec(memory_space=vm),) * 3,
        )(filtered, totals)

    in_specs = (P("band", "domain"), P("domain"), P("domain"), P(None, "domain"), P("domain"))
    out_specs = (P("band", "domain"), P("band", None), P("band", None))
    return jax.shard_map(
        per_device, mesh=mesh, in_specs=in_specs, out_specs=out_specs, check_vma=False
    )
```

```python
import math

import jax
import jax.numpy as jnp
import numpy as np
from jax import lax
from jax.experimental import pallas as pl
from jax.experimental.pallas import tpu as pltpu
from jax.sharding import PartitionSpec as P

DEG = 4
CENTRE = 5.0
SPREAD = 4.0
MESH = pl.DeviceIdType.MESH
F32 = jnp.float32
BF16 = jnp.bfloat16
F8 = jnp.float8_e4m3fn
PIECES = 4
STEP = 32.0
TOP = 128.0
LOC = 128
CHUNK = 512


def gauss_rule():
    inner = math.sqrt(5.0 - 2.0 * math.sqrt(10.0 / 7.0)) / 3.0
    outer = math.sqrt(5.0 + 2.0 * math.sqrt(10.0 / 7.0)) / 3.0
    w_inner = (322.0 + 13.0 * math.sqrt(70.0)) / 900.0
    w_outer = (322.0 - 13.0 * math.sqrt(70.0)) / 900.0
    points = np.array([-outer, -inner, 0.0, inner, outer])
    weights = np.array([w_outer, w_inner, 128.0 / 225.0, w_inner, w_outer])
    return (points, weights)


def element_matrix():
    nodes_1d = np.linspace(0.0, 1.0, 5)
    points, weights = gauss_rule()
    points = 0.5 * (points + 1.0)
    weights = 0.5 * weights
    values = np.ones((5, 5))
    slopes = np.zeros((5, 5))
    for i in range(5):
        for j in range(5):
            if j != i:
                values[i] = values[i] * (points - nodes_1d[j]) / (nodes_1d[i] - nodes_1d[j])
                product_term = np.ones(5) / (nodes_1d[i] - nodes_1d[j])
                for m in range(5):
                    if m != i and m != j:
                        product_term = (
                            product_term * (points - nodes_1d[m]) / (nodes_1d[i] - nodes_1d[m])
                        )
                slopes[i] = slopes[i] + product_term
    mass_1d = values * weights @ values.T
    stiffness = slopes * weights @ slopes.T
    whole = (
        np.kron(np.kron(stiffness, mass_1d), mass_1d)
        + np.kron(np.kron(mass_1d, stiffness), mass_1d)
        + np.kron(np.kron(mass_1d, mass_1d), stiffness)
    )
    return whole / np.max(np.sum(np.abs(whole), axis=1))


def element_tile():
    matrix = np.zeros((LOC, LOC), np.float32)
    matrix[:125, :125] = element_matrix().T.astype(np.float32)
    high = matrix.astype(jnp.bfloat16)
    low = (matrix - high.astype(np.float32)).astype(jnp.bfloat16)
    row = np.concatenate([high, low], axis=1)
    return np.concatenate([row, row], axis=0)


def dot(a, b):
    return jnp.dot(a, b, preferred_element_type=F32)


def row_max(x):
    return jnp.maximum(jnp.max(jnp.abs(x), axis=1, keepdims=True), 1e-30)


def cut(x, inverse):
    rest = x * inverse
    pieces = []
    for p in range(PIECES):
        piece = rest.astype(F8)
        pieces.append(piece)
        if p < PIECES - 1:
            rest = (rest - piece.astype(F32)) * STEP
    return pieces


def joined(d, scale, states):
    total = d[(PIECES - 1) * states :]
    for p in range(PIECES - 2, -1, -1):
        total = d[p * states : (p + 1) * states] + total * (1.0 / STEP)
    return total * scale


def kernel(
    n_domain, n_band, nodes_total,
    orb, pot, scl, conn, bnd, kk,
    filt_out, total_out,
    gt, gs, gpt, gps, bt, bs, pack, packp,
    cur, old, ay, pv, pb, pg, pr, pw, pwp, wo, xs, xsp, r2,
    bsend, grecv, rsend, rrecv,
    fall, lhs, rhs, part, rsrecv, zbuf, tot,
    out_s, pk_ss, pk_rs, b_ss, b_rs, r_ss, r_rs, f_ss, f_rs, s1_ss, s1_rs, s2_ss, s2_rs, s3_ss, s3_rs,
):
    states, nodes = orb.shape
    cells = conn.shape[0]
    ghosts = bnd.shape[0] * bnd.shape[1]
    width = cells * LOC
    me = lax.axis_index("domain")
    mb = lax.axis_index("band")
    nxt = lax.rem(me + 1, n_domain)
    prv = lax.rem(me + n_domain - 1, n_domain)
    near = mb + 1 - 2 * lax.rem(mb, 2)
    far = lax.rem(mb + 2, n_band)
    q = lax.rem(me, 8)
    z = me // 8
    zs = n_domain // 8
    base = z * 8

    barrier = pltpu.get_barrier_semaphore()

    def greet(where):
        pl.semaphore_signal(barrier, inc=1, device_id=where, device_id_type=MESH)

    greet({"domain": nxt})
    greet({"domain": prv})
    greet({"band": near})
    greet({"band": far})
    for r in range(1, 8):
        greet({"domain": base + lax.rem(q + r, 8)})
    for r in range(1, zs):
        greet({"domain": lax.rem(z + r, zs) * 8 + q})
    greeted = 4 + 7 + zs - 1

    def copy(src, dst, ss, rs, where):
        return pltpu.make_async_remote_copy(
            src_ref=src, dst_ref=dst, send_sem=ss, recv_sem=rs, device_id=where, device_id_type=MESH
        )

    pack[0:cells, :] = jnp.full((cells, LOC), -1.0, F32)
    pack[0:cells, 0 : conn.shape[1]] = conn[...].astype(F32)
    eye = lax.broadcasted_iota(jnp.int32, (cells, cells), 0) == lax.broadcasted_iota(
        jnp.int32, (cells, cells), 1
    )
    factors = jnp.sum(jnp.where(eye, scl[...], 0.0), axis=1, keepdims=True) * 0.5
    pack[cells : 2 * cells, :] = jnp.broadcast_to(factors, (cells, LOC))

    down = lax.broadcasted_iota(jnp.int32, (LOC, LOC), 0).astype(F32)
    across = lax.broadcasted_iota(jnp.int32, (LOC, LOC), 1).astype(F32)
    nothing = jnp.zeros((LOC, LOC), F8)

    def one_hot(upright, flat, span, row, first, count):
        block = jnp.floor(row * (1.0 / LOC))
        rest = jnp.broadcast_to(row - block * LOC, (LOC, LOC))
        block = jnp.broadcast_to(block, (LOC, LOC))
        hot_u = jnp.where(rest == down, 1.0, 0.0).astype(F8)
        hot_f = jnp.where(rest.T == across, 1.0, 0.0).astype(F8)
        block_u = block.astype(jnp.int32).astype(jnp.int8)
        block_f = block.T.astype(jnp.int32).astype(jnp.int8)
        for t in range(count // LOC):
            at = slice(t * LOC, (t + 1) * LOC)
            now = jnp.int8(first // LOC + t)
            upright[at, span] = jnp.where(block_u == now, hot_u, nothing)
            flat[span, at] = jnp.where(block_f == now, hot_f, nothing)

    def own_matrices(lo, hi):
        @pl.loop(lo, hi, unroll=4)
        def _(c):
            span = pl.ds(pl.multiple_of(c * LOC, LOC), LOC)
            one_hot(gt, gs, span, pack[pl.ds(c, 1), :], 0, nodes + ghosts)

    for g in range(ghosts // LOC):
        one_hot(bt, bs, slice(g * LOC, (g + 1) * LOC), bnd[g : g + 1, :].astype(F32), 0, nodes)
    own_matrices(0, cells // 2)
    pl.semaphore_wait(barrier, greeted)
    pack_copy = copy(pack, packp, pk_ss, pk_rs, {"domain": nxt})
    pack_copy.start()
    own_matrices(cells // 2, cells)

    cur[...] = orb[...]
    old[...] = orb[...]

    def put(dst, at, pieces):
        for p in range(PIECES):
            dst[p * states : (p + 1) * states, at] = pieces[p]

    def gathered(values, upright, rows, scale, dst):
        for n in range(0, width, CHUNK):
            u = joined(dot(values[...], upright[rows, n : n + CHUNK]), scale, states)
            for i in range(CHUNK // LOC):
                one = u[:, i * LOC : (i + 1) * LOC]
                high = one.astype(BF16)
                at = slice((n // LOC + i) * states, (n // LOC + i + 1) * states)
                dst[at, 0:LOC] = high
                dst[at, LOC : 2 * LOC] = (one - high.astype(F32)).astype(BF16)

    def cell_products(src, factor_rows, use):
        for c0 in range(0, cells, 8):
            both = dot(src[c0 * states : (c0 + 8) * states, :], kk[...])
            for i in range(8):
                at = slice(i * states, (i + 1) * states)
                use(
                    slice((c0 + i) * LOC, (c0 + i + 1) * LOC),
                    (both[at, 0:LOC] + both[at, LOC:]) * factor_rows[c0 + i : c0 + i + 1, :],
                )

    own = pack.at[cells : 2 * cells, :]
    before = packp.at[cells : 2 * cells, :]
    f_near = copy(fall.at[mb], fall.at[mb], f_ss.at[0], f_rs.at[0], {"band": near})
    halves = [slice(0, nodes // 2), slice(nodes // 2, nodes)]
    f_far = [
        copy(fall.at[mb, :, h], fall.at[mb, :, h], f_ss.at[1 + i], f_rs.at[1 + i], {"band": far})
        for i, h in enumerate(halves)
    ]
    f_pass = [
        copy(fall.at[far, :, h], fall.at[far, :, h], f_ss.at[3 + i], f_rs.at[3 + i], {"band": near})
        for i, h in enumerate(halves)
    ]

    def border_copy(k):
        return copy(bsend.at[k], grecv.at[k], b_ss.at[k], b_rs.at[k], {"domain": prv})

    def back_copy(k):
        return copy(rsend.at[k], rrecv.at[k], r_ss.at[k], r_rs.at[k], {"domain": nxt})

    f_out = pltpu.make_async_copy(fall.at[mb], filt_out, out_s)

    @pl.loop(0, DEG + 1)
    def _(k):
        y = cur[...]
        top = row_max(y)
        scale, inverse = top * (1.0 / TOP), TOP / top
        put(pv, slice(0, nodes), cut(y, inverse))
        d = dot(pv[...], bt[...])
        pb[...] = d.astype(F8)
        bsend[k] = joined(d, scale, states)
        border_copy(k).start()

        @pl.when(k == DEG)
        def _():
            fall[mb] = cur[...]
            f_near.start()
            f_far[0].start()
            f_far[1].start()
            f_out.start()

        gathered(pv, gt, slice(0, nodes), scale, xs)

        def keep(at, w):
            wo[:, at] = w
            put(pw, at, cut(w, inverse))

        cell_products(xs, own, keep)
        rsend[k] = joined(dot(pw[...], gs[:, nodes:]), scale, states)
        back_copy(k).start()

        @pl.when(k == 0)
        def _():
            pack_copy.wait()

            @pl.loop(0, cells, unroll=4)
            def _(c):
                span = pl.ds(pl.multiple_of(c * LOC, LOC), LOC)
                one_hot(gpt, gps, span, packp[pl.ds(c, 1), :], nodes, ghosts)

        gathered(pb, gpt, slice(0, ghosts), scale, xsp)
        cell_products(xsp, before, lambda at, w: put(pwp, at, cut(w, inverse)))
        r2[...] = joined(dot(pwp[...], gps[...]), scale, states)

        border_copy(k).wait_recv()
        ghost = grecv[k]
        top_g = row_max(ghost)
        scale_g, inverse_g = top_g * (1.0 / TOP), TOP / top_g
        put(pg, slice(0, ghosts), cut(ghost, inverse_g))
        both = jnp.maximum(top, top_g)
        scale_b, inverse_b = both * (1.0 / TOP), TOP / both
        gathered(pg, gt, slice(nodes, nodes + ghosts), scale_g, xs)
        cell_products(xs, own, lambda at, w: put(pw, at, cut(wo[:, at] + w, inverse_b)))
        for n in range(0, nodes, CHUNK):
            at = slice(n, n + CHUNK)
            ay[:, at] = joined(dot(pw[...], gs[:, at]), scale_b, states)

        @pl.when(k == DEG)
        def _():
            f_far[0].wait_recv()
            f_pass[0].start()

        back_copy(k).wait_recv()
        shared = rrecv[k] + r2[...]
        top_r = row_max(shared)
        put(pr, slice(0, ghosts), cut(shared, TOP / top_r))
        first = (k == 0).astype(F32)
        alpha = (2.0 - first) / SPREAD
        beta = 1.0 - first
        for n in range(0, nodes, CHUNK):
            h = joined(dot(pr[...], bs[:, n : n + CHUNK]), top_r * (1.0 / TOP), states)
            for i in range(CHUNK // LOC):
                at = slice(n + i * LOC, n + (i + 1) * LOC)
                t = n // LOC + i
                v = cur[:, at]
                full = ay[:, at] + h[:, i * LOC : (i + 1) * LOC] + pot[t : t + 1, :] * v
                ay[:, at] = full
                cur[:, at] = alpha * (full - CENTRE * v) - beta * old[:, at]
                old[:, at] = v

    f_far[1].wait_recv()
    f_pass[1].start()
    for i, value in enumerate((old, ay)):
        v = value[...]
        high = v.astype(BF16)
        lhs[2 * i * states : (2 * i + 1) * states, :] = high
        lhs[(2 * i + 1) * states : (2 * i + 2) * states, :] = (v - high.astype(F32)).astype(BF16)
    f_near.wait_recv()
    f_pass[0].wait_recv()
    f_pass[1].wait_recv()
    everyone = n_band * states
    for j in range(n_band):
        v = fall[j]
        high = v.astype(BF16)
        rhs[j * states : (j + 1) * states, :] = high
        rhs[everyone + j * states : everyone + (j + 1) * states, :] = (v - high.astype(F32)).astype(BF16)
    g = lax.dot_general(
        lhs[...], rhs[...], (((1,), (1,)), ((), ())), preferred_element_type=F32
    )
    g = g[:, :everyone] + g[:, everyone:]
    part[0 : states // 8] = (g[0:states] + g[states : 2 * states]).reshape(states // 8, 8, everyone)
    part[states // 8 :] = (g[2 * states : 3 * states] + g[3 * states :]).reshape(
        states // 8, 8, everyone
    )

    sends, sent = [], []
    for r in range(1, 8):
        peer = lax.rem(q + r, 8)
        c = copy(part.at[peer], rsrecv.at[r], s1_ss.at[r], s1_rs.at[r], {"domain": base + peer})
        c.start()
        sends.append(c)
    for c in sends:
        c.wait_recv()
    sent += sends
    total = part[q]
    for r in range(1, 8):
        total = total + rsrecv[r]
    zbuf[z] = total
    sends = []
    for r in range(1, zs):
        peer = lax.rem(z + r, zs)
        c = copy(zbuf.at[z], zbuf.at[z], s2_ss.at[r], s2_rs.at[r], {"domain": peer * 8 + q})
        c.start()
        sends.append(c)
    for c in sends:
        c.wait_recv()
    sent += sends
    total = zbuf[0]
    for r in range(1, zs):
        total = total + zbuf[r]
    tot[q] = total * (1.0 / nodes_total)
    sends = []
    for r in range(1, 8):
        peer = lax.rem(q + r, 8)
        c = copy(tot.at[q], tot.at[q], s3_ss.at[r], s3_rs.at[r], {"domain": base + peer})
        c.start()
        sends.append(c)
    for c in sends:
        c.wait_recv()
    sent += sends
    total_out[...] = tot[...].reshape(2 * states, everyone)
    for k in range(DEG + 1):
        border_copy(k).wait_send()
        back_copy(k).wait_send()
    for c in sent + [f_near] + f_far + f_pass:
        c.wait_send()
    f_out.wait()


def write_out(filt, total, filt_out, inter_out, proj_out):
    states = filt.shape[0]
    filt_out[...] = filt[...]
    inter_out[...] = total[0:states, :]
    proj_out[...] = total[states:, :]


def solution(mesh):
    n_domain, n_band = mesh.shape["domain"], mesh.shape["band"]
    tile = element_tile()

    def per_device(orbitals, potential, cell_scale, connectivity, boundary):
        states, nodes = orbitals.shape
        cells = connectivity.shape[1]
        ghosts = boundary.shape[0]
        width = cells * LOC
        rows = PIECES * states
        everyone = n_band * states
        vm = pltpu.VMEM
        dma = pltpu.SemaphoreType.DMA
        body = lambda *refs: kernel(n_domain, n_band, nodes * n_domain, *refs)
        filtered, totals = pl.pallas_call(
            body,
            name="chebyshev_step",
            out_shape=(
                jax.ShapeDtypeStruct((states, nodes), F32),
                jax.ShapeDtypeStruct((2 * states, everyone), F32),
            ),
            in_specs=[pl.BlockSpec(memory_space=vm)] * 6,
            out_specs=(pl.BlockSpec(memory_space=pl.ANY), pl.BlockSpec(memory_space=vm)),
            scratch_shapes=[
                vm((nodes + ghosts, width), F8),
                vm((width, nodes + ghosts), F8),
                vm((ghosts, width), F8),
                vm((width, ghosts), F8),
                vm((nodes, ghosts), F8),
                vm((ghosts, nodes), F8),
                vm((2 * cells, LOC), F32),
                vm((2 * cells, LOC), F32),
                vm((states, nodes), F32),
                vm((states, nodes), F32),
                vm((states, nodes), F32),
                vm((rows, nodes), F8),
                vm((rows, ghosts), F8),
                vm((rows, ghosts), F8),
                vm((rows, ghosts), F8),
                vm((rows, width), F8),
                vm((rows, width), F8),
                vm((states, width), F32),
                vm((cells * states, 2 * LOC), BF16),
                vm((cells * states, 2 * LOC), BF16),
                vm((states, ghosts), F32),
                vm((DEG + 1, states, ghosts), F32),
                vm((DEG + 1, states, ghosts), F32),
                vm((DEG + 1, states, ghosts), F32),
                vm((DEG + 1, states, ghosts), F32),
                vm((n_band, states, nodes), F32),
                vm((4 * states, nodes), BF16),
                vm((2 * everyone, nodes), BF16),
                vm((8, 8, everyone), F32),
                vm((8, 8, everyone), F32),
                vm((n_domain // 8, 8, everyone), F32),
                vm((8, 8, everyone), F32),
                dma, dma, dma,
                dma((DEG + 1,)), dma((DEG + 1,)), dma((DEG + 1,)), dma((DEG + 1,)),
                dma((5,)), dma((5,)),
                dma((8,)), dma((8,)), dma((n_domain // 8,)), dma((n_domain // 8,)), dma((8,)), dma((8,)),
            ],
            compiler_params=pltpu.CompilerParams(
                collective_id=0, has_side_effects=True, vmem_limit_bytes=60 * 2**20
            ),
        )(
            orbitals,
            potential.reshape(nodes // LOC, LOC),
            cell_scale.reshape(1, cells),
            connectivity.T,
            boundary.reshape(ghosts // LOC, LOC),
            jnp.asarray(tile),
        )
        return pl.pallas_call(
            write_out,
            name="outputs",
            out_shape=(
                jax.ShapeDtypeStruct((states, nodes), F32),
                jax.ShapeDtypeStruct((states, everyone), F32),
                jax.ShapeDtypeStruct((states, everyone), F32),
            ),
            in_specs=[pl.BlockSpec(memory_space=vm)] * 2,
            out_specs=(pl.BlockSpec(memory_space=vm),) * 3,
        )(filtered, totals)

    in_specs = (P("band", "domain"), P("domain"), P("domain"), P(None, "domain"), P("domain"))
    out_specs = (P("band", "domain"), P("band", None), P("band", None))
    return jax.shard_map(
        per_device, mesh=mesh, in_specs=in_specs, out_specs=out_specs, check_vma=False
    )
```

```python
import math

import jax
import jax.numpy as jnp
import numpy as np
from jax import lax
from jax.experimental import pallas as pl
from jax.experimental.pallas import tpu as pltpu
from jax.sharding import PartitionSpec as P

DEG = 4
CENTRE = 5.0
SPREAD = 4.0
MESH = pl.DeviceIdType.MESH
F32 = jnp.float32
BF16 = jnp.bfloat16
F8 = jnp.float8_e4m3fn
PIECES = 4
PRODUCT_PIECES = 3
STEP = 32.0
TOP = 128.0
LOC = 128
CHUNK = 512
PART = 8


def gauss_rule():
    inner = math.sqrt(5.0 - 2.0 * math.sqrt(10.0 / 7.0)) / 3.0
    outer = math.sqrt(5.0 + 2.0 * math.sqrt(10.0 / 7.0)) / 3.0
    w_inner = (322.0 + 13.0 * math.sqrt(70.0)) / 900.0
    w_outer = (322.0 - 13.0 * math.sqrt(70.0)) / 900.0
    points = np.array([-outer, -inner, 0.0, inner, outer])
    weights = np.array([w_outer, w_inner, 128.0 / 225.0, w_inner, w_outer])
    return (points, weights)


def element_matrix():
    nodes_1d = np.linspace(0.0, 1.0, 5)
    points, weights = gauss_rule()
    points = 0.5 * (points + 1.0)
    weights = 0.5 * weights
    values = np.ones((5, 5))
    slopes = np.zeros((5, 5))
    for i in range(5):
        for j in range(5):
            if j != i:
                values[i] = values[i] * (points - nodes_1d[j]) / (nodes_1d[i] - nodes_1d[j])
                product_term = np.ones(5) / (nodes_1d[i] - nodes_1d[j])
                for m in range(5):
                    if m != i and m != j:
                        product_term = (
                            product_term * (points - nodes_1d[m]) / (nodes_1d[i] - nodes_1d[m])
                        )
                slopes[i] = slopes[i] + product_term
    mass_1d = values * weights @ values.T
    stiffness = slopes * weights @ slopes.T
    whole = (
        np.kron(np.kron(stiffness, mass_1d), mass_1d)
        + np.kron(np.kron(mass_1d, stiffness), mass_1d)
        + np.kron(np.kron(mass_1d, mass_1d), stiffness)
    )
    return whole / np.max(np.sum(np.abs(whole), axis=1))


def element_tile():
    matrix = np.zeros((LOC, LOC), np.float32)
    matrix[:125, :125] = element_matrix().T.astype(np.float32)
    high = matrix.astype(jnp.bfloat16)
    low = (matrix - high.astype(np.float32)).astype(jnp.bfloat16)
    row = np.concatenate([high, low], axis=1)
    return np.concatenate([row, row], axis=0)


def dot(a, b):
    return jnp.dot(a, b, preferred_element_type=F32)


def row_max(x):
    return jnp.maximum(jnp.max(jnp.abs(x), axis=1, keepdims=True), 1e-30)


def cut(x, count):
    pieces = []
    for p in range(count):
        piece = x.astype(F8)
        pieces.append(piece)
        if p < count - 1:
            x = (x - piece.astype(F32)) * STEP
    return pieces


def joined(d, count):
    states = d.shape[0] // count
    total = d[(count - 1) * states :]
    for p in range(count - 2, -1, -1):
        total = d[p * states : (p + 1) * states] + total * (1.0 / STEP)
    return total


def kernel(
    n_domain, n_band, nodes_total,
    orb, pot, scl, conn, bnd, kk,
    filt_out, total_out,
    gt, gs, gpt, gps, bt, bs, pack, packp,
    cur, old, ay, pv, pb, pg, pr, pw, pwp, wo, xs, xsp, r2,
    bsend, grecv, rsend, rrecv,
    fall, lhs, rhs, part, rsrecv, zbuf, tot,
    out_s, pk_ss, pk_rs, b_ss, b_rs, r_ss, r_rs, f_ss, f_rs, s1_ss, s1_rs, s2_ss, s2_rs, s3_ss, s3_rs,
):
    states, nodes = orb.shape
    cells = conn.shape[0]
    ghosts = bnd.shape[0] * bnd.shape[1]
    width = cells * LOC
    me = lax.axis_index("domain")
    mb = lax.axis_index("band")
    nxt = lax.rem(me + 1, n_domain)
    prv = lax.rem(me + n_domain - 1, n_domain)
    near = mb + 1 - 2 * lax.rem(mb, 2)
    far = lax.rem(mb + 2, n_band)
    q = lax.rem(me, 8)
    z = me // 8
    zs = n_domain // 8
    base = z * 8

    barrier = pltpu.get_barrier_semaphore()

    def greet(where):
        pl.semaphore_signal(barrier, inc=1, device_id=where, device_id_type=MESH)

    greet({"domain": nxt})
    greet({"domain": prv})
    greet({"band": near})
    greet({"band": far})
    for r in range(1, 8):
        greet({"domain": base + lax.rem(q + r, 8)})
    for r in range(1, zs):
        greet({"domain": lax.rem(z + r, zs) * 8 + q})
    greeted = 4 + 7 + zs - 1

    def copy(src, dst, ss, rs, where):
        return pltpu.make_async_remote_copy(
            src_ref=src, dst_ref=dst, send_sem=ss, recv_sem=rs, device_id=where, device_id_type=MESH
        )

    pack[0:cells, :] = jnp.full((cells, LOC), -1.0, F32)
    pack[0:cells, 0 : conn.shape[1]] = conn[...].astype(F32)
    eye = lax.broadcasted_iota(jnp.int32, (cells, cells), 0) == lax.broadcasted_iota(
        jnp.int32, (cells, cells), 1
    )
    factors = jnp.sum(jnp.where(eye, scl[...], 0.0), axis=1, keepdims=True) * 0.5
    pack[cells : 2 * cells, :] = jnp.broadcast_to(factors, (cells, LOC))

    down = lax.broadcasted_iota(jnp.int32, (LOC, LOC), 0).astype(F32)
    across = lax.broadcasted_iota(jnp.int32, (LOC, LOC), 1).astype(F32)
    nothing = jnp.zeros((LOC, LOC), F8)

    def one_hot(upright, flat, span, row, first, count):
        block = jnp.floor(row * (1.0 / LOC))
        rest = jnp.broadcast_to(row - block * LOC, (LOC, LOC))
        block = jnp.broadcast_to(block, (LOC, LOC))
        hot_u = jnp.where(rest == down, 1.0, 0.0).astype(F8)
        hot_f = jnp.where(rest.T == across, 1.0, 0.0).astype(F8)
        block_u = block.astype(jnp.int32).astype(jnp.int8)
        block_f = block.T.astype(jnp.int32).astype(jnp.int8)
        for t in range(count // LOC):
            at = slice(t * LOC, (t + 1) * LOC)
            now = jnp.int8(first // LOC + t)
            upright[at, span] = jnp.where(block_u == now, hot_u, nothing)
            flat[span, at] = jnp.where(block_f == now, hot_f, nothing)

    def own_matrices(lo, hi):
        @pl.loop(lo, hi, unroll=4)
        def _(c):
            span = pl.ds(pl.multiple_of(c * LOC, LOC), LOC)
            one_hot(gt, gs, span, pack[pl.ds(c, 1), :], 0, nodes + ghosts)

    for g in range(ghosts // LOC):
        one_hot(bt, bs, slice(g * LOC, (g + 1) * LOC), bnd[g : g + 1, :].astype(F32), 0, nodes)
    own_matrices(0, cells // 2)
    pl.semaphore_wait(barrier, greeted)
    pack_copy = copy(pack, packp, pk_ss, pk_rs, {"domain": nxt})
    pack_copy.start()
    own_matrices(cells // 2, cells)

    cur[...] = orb[...]
    old[...] = orb[...]

    def put(dst, at, pieces):
        for p, piece in enumerate(pieces):
            dst[p * states : (p + 1) * states, at] = piece

    def gathered(values, upright, rows, dst, lo, hi):
        for n in range(lo * LOC, hi * LOC, CHUNK):
            u = joined(dot(values[...], upright[rows, n : n + CHUNK]), PIECES)
            for i in range(CHUNK // LOC):
                one = u[:, i * LOC : (i + 1) * LOC]
                high = one.astype(BF16)
                at = slice((n // LOC + i) * states, (n // LOC + i + 1) * states)
                dst[at, 0:LOC] = high
                dst[at, LOC : 2 * LOC] = (one - high.astype(F32)).astype(BF16)

    def cell_products(src, factor_rows, use, lo, hi):
        both = dot(src[lo * states : hi * states, :], kk[...])
        for i in range(hi - lo):
            at = slice(i * states, (i + 1) * states)
            use(
                slice((lo + i) * LOC, (lo + i + 1) * LOC),
                (both[at, 0:LOC] + both[at, LOC:]) * factor_rows[lo + i : lo + i + 1, :],
            )

    def elements(values, upright, rows, dst, factor_rows, use):
        gathered(values, upright, rows, dst, 0, cells)
        for c in range(0, cells, PART):
            cell_products(dst, factor_rows, use, c, c + PART)

    own = pack.at[cells : 2 * cells, :]
    before = packp.at[cells : 2 * cells, :]
    f_near = copy(fall.at[mb], fall.at[mb], f_ss.at[0], f_rs.at[0], {"band": near})
    halves = [slice(0, nodes // 2), slice(nodes // 2, nodes)]
    f_far = [
        copy(fall.at[mb, :, h], fall.at[mb, :, h], f_ss.at[1 + i], f_rs.at[1 + i], {"band": far})
        for i, h in enumerate(halves)
    ]
    f_pass = [
        copy(fall.at[far, :, h], fall.at[far, :, h], f_ss.at[3 + i], f_rs.at[3 + i], {"band": near})
        for i, h in enumerate(halves)
    ]

    def border_copy(k):
        return copy(bsend.at[k], grecv.at[k], b_ss.at[k], b_rs.at[k], {"domain": prv})

    def back_copy(k):
        return copy(rsend.at[k], rrecv.at[k], r_ss.at[k], r_rs.at[k], {"domain": nxt})

    f_out = pltpu.make_async_copy(fall.at[mb], filt_out, out_s)

    @pl.loop(0, DEG + 1)
    def _(k):
        y = cur[...]
        top = row_max(y)
        scale, inverse = top * (1.0 / TOP), TOP / top
        put(pv, slice(0, nodes), cut(y * inverse, PIECES))
        d = dot(pv[...], bt[...])
        pb[...] = d.astype(F8)
        bsend[k] = joined(d, PIECES) * scale
        border_copy(k).start()

        @pl.when(k == DEG)
        def _():
            fall[mb] = cur[...]
            f_near.start()
            f_far[0].start()
            f_far[1].start()
            f_out.start()

        def keep(at, w):
            wo[:, at] = w
            put(pw, at, cut(w, PRODUCT_PIECES))

        elements(pv, gt, slice(0, nodes), xs, own, keep)
        rsend[k] = joined(dot(pw[...], gs[:, nodes:]), PRODUCT_PIECES) * scale
        back_copy(k).start()

        @pl.when(k == 0)
        def _():
            pack_copy.wait()

            @pl.loop(0, cells, unroll=4)
            def _(c):
                span = pl.ds(pl.multiple_of(c * LOC, LOC), LOC)
                one_hot(gpt, gps, span, packp[pl.ds(c, 1), :], nodes, ghosts)

        elements(
            pb, gpt, slice(0, ghosts), xsp, before,
            lambda at, w: put(pwp, at, cut(w, PRODUCT_PIECES)),
        )
        r2[...] = joined(dot(pwp[...], gps[...]), PRODUCT_PIECES) * scale

        border_copy(k).wait_recv()
        ghost = grecv[k]
        top_g = row_max(ghost)
        put(pg, slice(0, ghosts), cut(ghost * (TOP / top_g), PIECES))
        both = jnp.maximum(top, top_g)
        ratio, ratio_g, scale_b = top / both, top_g / both, both * (1.0 / TOP)
        elements(
            pg, gt, slice(nodes, nodes + ghosts), xs, own,
            lambda at, w: put(pw, at, cut(wo[:, at] * ratio + w * ratio_g, PRODUCT_PIECES)),
        )
        for n in range(0, nodes, CHUNK):
            at = slice(n, n + CHUNK)
            ay[:, at] = joined(dot(pw[...], gs[:, at]), PRODUCT_PIECES) * scale_b

        @pl.when(k == DEG)
        def _():
            f_far[0].wait_recv()
            f_pass[0].start()

        back_copy(k).wait_recv()
        shared = rrecv[k] + r2[...]
        top_r = row_max(shared)
        put(pr, slice(0, ghosts), cut(shared * (TOP / top_r), PIECES))
        first = (k == 0).astype(F32)
        alpha = (2.0 - first) / SPREAD
        beta = 1.0 - first
        for n in range(0, nodes, CHUNK):
            h = joined(dot(pr[...], bs[:, n : n + CHUNK]), PIECES) * (top_r * (1.0 / TOP))
            for i in range(CHUNK // LOC):
                at = slice(n + i * LOC, n + (i + 1) * LOC)
                t = n // LOC + i
                v = cur[:, at]
                full = ay[:, at] + h[:, i * LOC : (i + 1) * LOC] + pot[t : t + 1, :] * v
                ay[:, at] = full
                cur[:, at] = alpha * (full - CENTRE * v) - beta * old[:, at]
                old[:, at] = v

    f_far[1].wait_recv()
    f_pass[1].start()
    for i, value in enumerate((old, ay)):
        v = value[...]
        high = v.astype(BF16)
        lhs[2 * i * states : (2 * i + 1) * states, :] = high
        lhs[(2 * i + 1) * states : (2 * i + 2) * states, :] = (v - high.astype(F32)).astype(BF16)
    f_near.wait_recv()
    f_pass[0].wait_recv()
    f_pass[1].wait_recv()
    everyone = n_band * states
    for j in range(n_band):
        v = fall[j]
        high = v.astype(BF16)
        rhs[j * states : (j + 1) * states, :] = high
        rhs[everyone + j * states : everyone + (j + 1) * states, :] = (v - high.astype(F32)).astype(BF16)
    g = lax.dot_general(
        lhs[...], rhs[...], (((1,), (1,)), ((), ())), preferred_element_type=F32
    )
    g = g[:, :everyone] + g[:, everyone:]
    part[0 : states // 8] = (g[0:states] + g[states : 2 * states]).reshape(states // 8, 8, everyone)
    part[states // 8 :] = (g[2 * states : 3 * states] + g[3 * states :]).reshape(
        states // 8, 8, everyone
    )

    sends, sent = [], []
    for r in range(1, 8):
        peer = lax.rem(q + r, 8)
        c = copy(part.at[peer], rsrecv.at[r], s1_ss.at[r], s1_rs.at[r], {"domain": base + peer})
        c.start()
        sends.append(c)
    for c in sends:
        c.wait_recv()
    sent += sends
    total = part[q]
    for r in range(1, 8):
        total = total + rsrecv[r]
    zbuf[z] = total
    sends = []
    for r in range(1, zs):
        peer = lax.rem(z + r, zs)
        c = copy(zbuf.at[z], zbuf.at[z], s2_ss.at[r], s2_rs.at[r], {"domain": peer * 8 + q})
        c.start()
        sends.append(c)
    for c in sends:
        c.wait_recv()
    sent += sends
    total = zbuf[0]
    for r in range(1, zs):
        total = total + zbuf[r]
    tot[q] = total * (1.0 / nodes_total)
    sends = []
    for r in range(1, 8):
        peer = lax.rem(q + r, 8)
        c = copy(tot.at[q], tot.at[q], s3_ss.at[r], s3_rs.at[r], {"domain": base + peer})
        c.start()
        sends.append(c)
    for c in sends:
        c.wait_recv()
    sent += sends
    total_out[...] = tot[...].reshape(2 * states, everyone)
    for k in range(DEG + 1):
        border_copy(k).wait_send()
        back_copy(k).wait_send()
    for c in sent + [f_near] + f_far + f_pass:
        c.wait_send()
    f_out.wait()


def write_out(filt, total, filt_out, inter_out, proj_out):
    states = filt.shape[0]
    filt_out[...] = filt[...]
    inter_out[...] = total[0:states, :]
    proj_out[...] = total[states:, :]


def solution(mesh):
    n_domain, n_band = mesh.shape["domain"], mesh.shape["band"]
    tile = element_tile()

    def per_device(orbitals, potential, cell_scale, connectivity, boundary):
        states, nodes = orbitals.shape
        cells = connectivity.shape[1]
        ghosts = boundary.shape[0]
        width = cells * LOC
        rows = PIECES * states
        everyone = n_band * states
        vm = pltpu.VMEM
        dma = pltpu.SemaphoreType.DMA
        body = lambda *refs: kernel(n_domain, n_band, nodes * n_domain, *refs)
        filtered, totals = pl.pallas_call(
            body,
            name="chebyshev_step",
            out_shape=(
                jax.ShapeDtypeStruct((states, nodes), F32),
                jax.ShapeDtypeStruct((2 * states, everyone), F32),
            ),
            in_specs=[pl.BlockSpec(memory_space=vm)] * 6,
            out_specs=(pl.BlockSpec(memory_space=pl.ANY), pl.BlockSpec(memory_space=vm)),
            scratch_shapes=[
                vm((nodes + ghosts, width), F8),
                vm((width, nodes + ghosts), F8),
                vm((ghosts, width), F8),
                vm((width, ghosts), F8),
                vm((nodes, ghosts), F8),
                vm((ghosts, nodes), F8),
                vm((2 * cells, LOC), F32),
                vm((2 * cells, LOC), F32),
                vm((states, nodes), F32),
                vm((states, nodes), F32),
                vm((states, nodes), F32),
                vm((rows, nodes), F8),
                vm((rows, ghosts), F8),
                vm((rows, ghosts), F8),
                vm((rows, ghosts), F8),
                vm((PRODUCT_PIECES * states, width), F8),
                vm((PRODUCT_PIECES * states, width), F8),
                vm((states, width), F32),
                vm((cells * states, 2 * LOC), BF16),
                vm((cells * states, 2 * LOC), BF16),
                vm((states, ghosts), F32),
                vm((DEG + 1, states, ghosts), F32),
                vm((DEG + 1, states, ghosts), F32),
                vm((DEG + 1, states, ghosts), F32),
                vm((DEG + 1, states, ghosts), F32),
                vm((n_band, states, nodes), F32),
                vm((4 * states, nodes), BF16),
                vm((2 * everyone, nodes), BF16),
                vm((8, 8, everyone), F32),
                vm((8, 8, everyone), F32),
                vm((n_domain // 8, 8, everyone), F32),
                vm((8, 8, everyone), F32),
                dma, dma, dma,
                dma((DEG + 1,)), dma((DEG + 1,)), dma((DEG + 1,)), dma((DEG + 1,)),
                dma((5,)), dma((5,)),
                dma((8,)), dma((8,)), dma((n_domain // 8,)), dma((n_domain // 8,)), dma((8,)), dma((8,)),
            ],
            compiler_params=pltpu.CompilerParams(
                collective_id=0, has_side_effects=True, vmem_limit_bytes=60 * 2**20
            ),
        )(
            orbitals,
            potential.reshape(nodes // LOC, LOC),
            cell_scale.reshape(1, cells),
            connectivity.T,
            boundary.reshape(ghosts // LOC, LOC),
            jnp.asarray(tile),
        )
        return pl.pallas_call(
            write_out,
            name="outputs",
            out_shape=(
                jax.ShapeDtypeStruct((states, nodes), F32),
                jax.ShapeDtypeStruct((states, everyone), F32),
                jax.ShapeDtypeStruct((states, everyone), F32),
            ),
            in_specs=[pl.BlockSpec(memory_space=vm)] * 2,
            out_specs=(pl.BlockSpec(memory_space=vm),) * 3,
        )(filtered, totals)

    in_specs = (P("band", "domain"), P("domain"), P("domain"), P(None, "domain"), P("domain"))
    out_specs = (P("band", "domain"), P("band", None), P("band", None))
    return jax.shard_map(
        per_device, mesh=mesh, in_specs=in_specs, out_specs=out_specs, check_vma=False
    )
```

```python
import math

import jax
import jax.numpy as jnp
import numpy as np
from jax import lax
from jax.experimental import pallas as pl
from jax.experimental.pallas import tpu as pltpu
from jax.sharding import PartitionSpec as P

DEG = 4
CENTRE = 5.0
SPREAD = 4.0
MESH = pl.DeviceIdType.MESH
F32 = jnp.float32
BF16 = jnp.bfloat16
F8 = jnp.float8_e4m3fn
PIECES = 4
PRODUCT_PIECES = 3
STEP = 32.0
TOP = 128.0
LOC = 128
CHUNK = 512
PART = 8


def gauss_rule():
    inner = math.sqrt(5.0 - 2.0 * math.sqrt(10.0 / 7.0)) / 3.0
    outer = math.sqrt(5.0 + 2.0 * math.sqrt(10.0 / 7.0)) / 3.0
    w_inner = (322.0 + 13.0 * math.sqrt(70.0)) / 900.0
    w_outer = (322.0 - 13.0 * math.sqrt(70.0)) / 900.0
    points = np.array([-outer, -inner, 0.0, inner, outer])
    weights = np.array([w_outer, w_inner, 128.0 / 225.0, w_inner, w_outer])
    return (points, weights)


def element_matrix():
    nodes_1d = np.linspace(0.0, 1.0, 5)
    points, weights = gauss_rule()
    points = 0.5 * (points + 1.0)
    weights = 0.5 * weights
    values = np.ones((5, 5))
    slopes = np.zeros((5, 5))
    for i in range(5):
        for j in range(5):
            if j != i:
                values[i] = values[i] * (points - nodes_1d[j]) / (nodes_1d[i] - nodes_1d[j])
                product_term = np.ones(5) / (nodes_1d[i] - nodes_1d[j])
                for m in range(5):
                    if m != i and m != j:
                        product_term = (
                            product_term * (points - nodes_1d[m]) / (nodes_1d[i] - nodes_1d[m])
                        )
                slopes[i] = slopes[i] + product_term
    mass_1d = values * weights @ values.T
    stiffness = slopes * weights @ slopes.T
    whole = (
        np.kron(np.kron(stiffness, mass_1d), mass_1d)
        + np.kron(np.kron(mass_1d, stiffness), mass_1d)
        + np.kron(np.kron(mass_1d, mass_1d), stiffness)
    )
    return whole / np.max(np.sum(np.abs(whole), axis=1))


def element_tile():
    matrix = np.zeros((LOC, LOC), np.float32)
    matrix[:125, :125] = element_matrix().T.astype(np.float32)
    high = matrix.astype(jnp.bfloat16)
    low = (matrix - high.astype(np.float32)).astype(jnp.bfloat16)
    row = np.concatenate([high, low], axis=1)
    return np.concatenate([row, row], axis=0)


def dot(a, b):
    return jnp.dot(a, b, preferred_element_type=F32)


def row_max(x):
    return jnp.maximum(jnp.max(jnp.abs(x), axis=1, keepdims=True), 1e-30)


def cut(x, count):
    pieces = []
    for p in range(count):
        piece = x.astype(F8)
        pieces.append(piece)
        if p < count - 1:
            x = (x - piece.astype(F32)) * STEP
    return pieces


def joined(d, count):
    states = d.shape[0] // count
    total = d[(count - 1) * states :]
    for p in range(count - 2, -1, -1):
        total = d[p * states : (p + 1) * states] + total * (1.0 / STEP)
    return total


def kernel(
    n_domain, n_band, nodes_total,
    orb_in, pot_in, scl_in, conn_in, bnd_in, kk_in,
    filt_out, total_out,
    gt, gs, gpt, gps, bt, bs, pack, packp,
    cur, old, ay, pv, pb, pg, pr, pw, pwp, wo, xs, xsp, r2,
    bsend, grecv, rsend, rrecv,
    fall, lhs, rhs, part, rsrecv, zbuf, tot, pot, scl, conn, bnd, kk, in_s,
    out_s, pk_ss, pk_rs, b_ss, b_rs, r_ss, r_rs, f_ss, f_rs, s1_ss, s1_rs, s2_ss, s2_rs, s3_ss, s3_rs,
):
    fetches = [
        pltpu.make_async_copy(src, dst, in_s.at[i])
        for i, (src, dst) in enumerate(
            (
                (conn_in, conn), (bnd_in, bnd), (scl_in, scl), (orb_in, cur),
                (orb_in, old), (kk_in, kk), (pot_in, pot),
            )
        )
    ]
    for fetch in fetches:
        fetch.start()
    states, nodes = orb_in.shape
    cells = conn.shape[0]
    ghosts = bnd.shape[0] * bnd.shape[1]
    width = cells * LOC
    me = lax.axis_index("domain")
    mb = lax.axis_index("band")
    nxt = lax.rem(me + 1, n_domain)
    prv = lax.rem(me + n_domain - 1, n_domain)
    near = mb + 1 - 2 * lax.rem(mb, 2)
    far = lax.rem(mb + 2, n_band)
    q = lax.rem(me, 8)
    z = me // 8
    zs = n_domain // 8
    base = z * 8

    barrier = pltpu.get_barrier_semaphore()

    def greet(where):
        pl.semaphore_signal(barrier, inc=1, device_id=where, device_id_type=MESH)

    greet({"domain": nxt})
    greet({"domain": prv})
    greet({"band": near})
    greet({"band": far})
    for r in range(1, 8):
        greet({"domain": base + lax.rem(q + r, 8)})
    for r in range(1, zs):
        greet({"domain": lax.rem(z + r, zs) * 8 + q})
    greeted = 4 + 7 + zs - 1

    def copy(src, dst, ss, rs, where):
        return pltpu.make_async_remote_copy(
            src_ref=src, dst_ref=dst, send_sem=ss, recv_sem=rs, device_id=where, device_id_type=MESH
        )

    for fetch in fetches[:3]:
        fetch.wait()
    pack[0:cells, :] = jnp.full((cells, LOC), -1.0, F32)
    pack[0:cells, 0 : conn.shape[1]] = conn[...].astype(F32)
    eye = lax.broadcasted_iota(jnp.int32, (cells, cells), 0) == lax.broadcasted_iota(
        jnp.int32, (cells, cells), 1
    )
    factors = jnp.sum(jnp.where(eye, scl[...], 0.0), axis=1, keepdims=True) * 0.5
    pack[cells : 2 * cells, :] = jnp.broadcast_to(factors, (cells, LOC))

    down = lax.broadcasted_iota(jnp.int32, (LOC, LOC), 0).astype(F32)
    across = lax.broadcasted_iota(jnp.int32, (LOC, LOC), 1).astype(F32)
    nothing = jnp.zeros((LOC, LOC), F8)

    def one_hot(upright, flat, span, row, first, count):
        block = jnp.floor(row * (1.0 / LOC))
        rest = jnp.broadcast_to(row - block * LOC, (LOC, LOC))
        block = jnp.broadcast_to(block, (LOC, LOC))
        hot_u = jnp.where(rest == down, 1.0, 0.0).astype(F8)
        hot_f = jnp.where(rest.T == across, 1.0, 0.0).astype(F8)
        block_u = block.astype(jnp.int32).astype(jnp.int8)
        block_f = block.T.astype(jnp.int32).astype(jnp.int8)
        for t in range(count // LOC):
            at = slice(t * LOC, (t + 1) * LOC)
            now = jnp.int8(first // LOC + t)
            upright[at, span] = jnp.where(block_u == now, hot_u, nothing)
            flat[span, at] = jnp.where(block_f == now, hot_f, nothing)

    def own_matrices(lo, hi):
        @pl.loop(lo, hi, unroll=4)
        def _(c):
            span = pl.ds(pl.multiple_of(c * LOC, LOC), LOC)
            one_hot(gt, gs, span, pack[pl.ds(c, 1), :], 0, nodes + ghosts)

    for g in range(ghosts // LOC):
        one_hot(bt, bs, slice(g * LOC, (g + 1) * LOC), bnd[g : g + 1, :].astype(F32), 0, nodes)
    own_matrices(0, cells // 2)
    pl.semaphore_wait(barrier, greeted)
    pack_copy = copy(pack, packp, pk_ss, pk_rs, {"domain": nxt})
    pack_copy.start()
    own_matrices(cells // 2, cells)

    for fetch in fetches[3:]:
        fetch.wait()

    def put(dst, at, pieces):
        for p, piece in enumerate(pieces):
            dst[p * states : (p + 1) * states, at] = piece

    def gathered(values, upright, rows, dst, lo, hi):
        for n in range(lo * LOC, hi * LOC, CHUNK):
            u = joined(dot(values[...], upright[rows, n : n + CHUNK]), PIECES)
            for i in range(CHUNK // LOC):
                one = u[:, i * LOC : (i + 1) * LOC]
                high = one.astype(BF16)
                at = slice((n // LOC + i) * states, (n // LOC + i + 1) * states)
                dst[at, 0:LOC] = high
                dst[at, LOC : 2 * LOC] = (one - high.astype(F32)).astype(BF16)

    def cell_products(src, factor_rows, use, lo, hi):
        both = dot(src[lo * states : hi * states, :], kk[...])
        for i in range(hi - lo):
            at = slice(i * states, (i + 1) * states)
            use(
                slice((lo + i) * LOC, (lo + i + 1) * LOC),
                (both[at, 0:LOC] + both[at, LOC:]) * factor_rows[lo + i : lo + i + 1, :],
            )

    def elements(values, upright, rows, dst, factor_rows, use):
        gathered(values, upright, rows, dst, 0, cells)
        for c in range(0, cells, PART):
            cell_products(dst, factor_rows, use, c, c + PART)

    own = pack.at[cells : 2 * cells, :]
    before = packp.at[cells : 2 * cells, :]
    f_near = copy(fall.at[mb], fall.at[mb], f_ss.at[0], f_rs.at[0], {"band": near})
    halves = [slice(0, nodes // 2), slice(nodes // 2, nodes)]
    f_far = [
        copy(fall.at[mb, :, h], fall.at[mb, :, h], f_ss.at[1 + i], f_rs.at[1 + i], {"band": far})
        for i, h in enumerate(halves)
    ]
    f_pass = [
        copy(fall.at[far, :, h], fall.at[far, :, h], f_ss.at[3 + i], f_rs.at[3 + i], {"band": near})
        for i, h in enumerate(halves)
    ]

    def border_copy(k):
        return copy(bsend.at[k], grecv.at[k], b_ss.at[k], b_rs.at[k], {"domain": prv})

    def back_copy(k):
        return copy(rsend.at[k], rrecv.at[k], r_ss.at[k], r_rs.at[k], {"domain": nxt})

    f_out = pltpu.make_async_copy(fall.at[mb], filt_out, out_s)

    @pl.loop(0, DEG + 1)
    def _(k):
        y = cur[...]
        top = row_max(y)
        scale, inverse = top * (1.0 / TOP), TOP / top
        put(pv, slice(0, nodes), cut(y * inverse, PIECES))
        d = dot(pv[...], bt[...])
        pb[...] = d.astype(F8)
        bsend[k] = joined(d, PIECES) * scale
        border_copy(k).start()

        @pl.when(k == DEG)
        def _():
            fall[mb] = cur[...]
            f_near.start()
            f_far[0].start()
            f_out.start()

        def keep(at, w):
            wo[:, at] = w
            put(pw, at, cut(w, PRODUCT_PIECES))

        elements(pv, gt, slice(0, nodes), xs, own, keep)
        rsend[k] = joined(dot(pw[...], gs[:, nodes:]), PRODUCT_PIECES) * scale
        back_copy(k).start()

        @pl.when(k == DEG)
        def _():
            f_far[1].start()

        @pl.when(k == 0)
        def _():
            pack_copy.wait()

            @pl.loop(0, cells, unroll=4)
            def _(c):
                span = pl.ds(pl.multiple_of(c * LOC, LOC), LOC)
                one_hot(gpt, gps, span, packp[pl.ds(c, 1), :], nodes, ghosts)

        elements(
            pb, gpt, slice(0, ghosts), xsp, before,
            lambda at, w: put(pwp, at, cut(w, PRODUCT_PIECES)),
        )
        r2[...] = joined(dot(pwp[...], gps[...]), PRODUCT_PIECES) * scale

        border_copy(k).wait_recv()
        ghost = grecv[k]
        top_g = row_max(ghost)
        put(pg, slice(0, ghosts), cut(ghost * (TOP / top_g), PIECES))
        both = jnp.maximum(top, top_g)
        ratio, ratio_g, scale_b = top / both, top_g / both, both * (1.0 / TOP)
        elements(
            pg, gt, slice(nodes, nodes + ghosts), xs, own,
            lambda at, w: put(pw, at, cut(wo[:, at] * ratio + w * ratio_g, PRODUCT_PIECES)),
        )
        for n in range(0, nodes, CHUNK):
            at = slice(n, n + CHUNK)
            ay[:, at] = joined(dot(pw[...], gs[:, at]), PRODUCT_PIECES) * scale_b

        @pl.when(k == DEG)
        def _():
            f_far[0].wait_recv()
            f_pass[0].start()

        back_copy(k).wait_recv()
        shared = rrecv[k] + r2[...]
        top_r = row_max(shared)
        put(pr, slice(0, ghosts), cut(shared * (TOP / top_r), PIECES))
        first = (k == 0).astype(F32)
        alpha = (2.0 - first) / SPREAD
        beta = 1.0 - first
        for n in range(0, nodes, CHUNK):
            h = joined(dot(pr[...], bs[:, n : n + CHUNK]), PIECES) * (top_r * (1.0 / TOP))
            for i in range(CHUNK // LOC):
                at = slice(n + i * LOC, n + (i + 1) * LOC)
                t = n // LOC + i
                v = cur[:, at]
                full = ay[:, at] + h[:, i * LOC : (i + 1) * LOC] + pot[t : t + 1, :] * v
                ay[:, at] = full
                cur[:, at] = alpha * (full - CENTRE * v) - beta * old[:, at]
                old[:, at] = v

    f_far[1].wait_recv()
    f_pass[1].start()
    for i, value in enumerate((old, ay)):
        v = value[...]
        high = v.astype(BF16)
        lhs[2 * i * states : (2 * i + 1) * states, :] = high
        lhs[(2 * i + 1) * states : (2 * i + 2) * states, :] = (v - high.astype(F32)).astype(BF16)
    f_near.wait_recv()
    f_pass[0].wait_recv()
    f_pass[1].wait_recv()
    everyone = n_band * states
    for j in range(n_band):
        v = fall[j]
        high = v.astype(BF16)
        rhs[j * states : (j + 1) * states, :] = high
        rhs[everyone + j * states : everyone + (j + 1) * states, :] = (v - high.astype(F32)).astype(BF16)
    g = lax.dot_general(
        lhs[...], rhs[...], (((1,), (1,)), ((), ())), preferred_element_type=F32
    )
    g = g[:, :everyone] + g[:, everyone:]
    part[0 : states // 8] = (g[0:states] + g[states : 2 * states]).reshape(states // 8, 8, everyone)
    part[states // 8 :] = (g[2 * states : 3 * states] + g[3 * states :]).reshape(
        states // 8, 8, everyone
    )

    sends, sent = [], []
    for r in range(1, 8):
        peer = lax.rem(q + r, 8)
        c = copy(part.at[peer], rsrecv.at[r], s1_ss.at[r], s1_rs.at[r], {"domain": base + peer})
        c.start()
        sends.append(c)
    for c in sends:
        c.wait_recv()
    sent += sends
    total = part[q]
    for r in range(1, 8):
        total = total + rsrecv[r]
    zbuf[z] = total
    sends = []
    for r in range(1, zs):
        peer = lax.rem(z + r, zs)
        c = copy(zbuf.at[z], zbuf.at[z], s2_ss.at[r], s2_rs.at[r], {"domain": peer * 8 + q})
        c.start()
        sends.append(c)
    for c in sends:
        c.wait_recv()
    sent += sends
    total = zbuf[0]
    for r in range(1, zs):
        total = total + zbuf[r]
    tot[q] = total * (1.0 / nodes_total)
    sends = []
    for r in range(1, 8):
        peer = lax.rem(q + r, 8)
        c = copy(tot.at[q], tot.at[q], s3_ss.at[r], s3_rs.at[r], {"domain": base + peer})
        c.start()
        sends.append(c)
    for c in sends:
        c.wait_recv()
    sent += sends
    total_out[...] = tot[...].reshape(2 * states, everyone)
    for k in range(DEG + 1):
        border_copy(k).wait_send()
        back_copy(k).wait_send()
    for c in sent + [f_near] + f_far + f_pass:
        c.wait_send()
    f_out.wait()


def write_out(filt, total, filt_out, inter_out, proj_out):
    states = filt.shape[0]
    filt_out[...] = filt[...]
    inter_out[...] = total[0:states, :]
    proj_out[...] = total[states:, :]


def solution(mesh):
    n_domain, n_band = mesh.shape["domain"], mesh.shape["band"]
    tile = element_tile()

    def per_device(orbitals, potential, cell_scale, connectivity, boundary):
        states, nodes = orbitals.shape
        cells = connectivity.shape[1]
        ghosts = boundary.shape[0]
        width = cells * LOC
        rows = PIECES * states
        everyone = n_band * states
        vm = pltpu.VMEM
        dma = pltpu.SemaphoreType.DMA
        body = lambda *refs: kernel(n_domain, n_band, nodes * n_domain, *refs)
        filtered, totals = pl.pallas_call(
            body,
            name="chebyshev_step",
            out_shape=(
                jax.ShapeDtypeStruct((states, nodes), F32),
                jax.ShapeDtypeStruct((2 * states, everyone), F32),
            ),
            in_specs=[pl.BlockSpec(memory_space=pl.ANY)] * 6,
            out_specs=(pl.BlockSpec(memory_space=pl.ANY), pl.BlockSpec(memory_space=vm)),
            scratch_shapes=[
                vm((nodes + ghosts, width), F8),
                vm((width, nodes + ghosts), F8),
                vm((ghosts, width), F8),
                vm((width, ghosts), F8),
                vm((nodes, ghosts), F8),
                vm((ghosts, nodes), F8),
                vm((2 * cells, LOC), F32),
                vm((2 * cells, LOC), F32),
                vm((states, nodes), F32),
                vm((states, nodes), F32),
                vm((states, nodes), F32),
                vm((rows, nodes), F8),
                vm((rows, ghosts), F8),
                vm((rows, ghosts), F8),
                vm((rows, ghosts), F8),
                vm((PRODUCT_PIECES * states, width), F8),
                vm((PRODUCT_PIECES * states, width), F8),
                vm((states, width), F32),
                vm((cells * states, 2 * LOC), BF16),
                vm((cells * states, 2 * LOC), BF16),
                vm((states, ghosts), F32),
                vm((DEG + 1, states, ghosts), F32),
                vm((DEG + 1, states, ghosts), F32),
                vm((DEG + 1, states, ghosts), F32),
                vm((DEG + 1, states, ghosts), F32),
                vm((n_band, states, nodes), F32),
                vm((4 * states, nodes), BF16),
                vm((2 * everyone, nodes), BF16),
                vm((8, 8, everyone), F32),
                vm((8, 8, everyone), F32),
                vm((n_domain // 8, 8, everyone), F32),
                vm((8, 8, everyone), F32),
                vm((nodes // LOC, LOC), F32),
                vm((1, cells), F32),
                vm((cells, connectivity.shape[0]), jnp.int32),
                vm((ghosts // LOC, LOC), jnp.int32),
                vm((2 * LOC, 2 * LOC), BF16),
                dma((7,)),
                dma, dma, dma,
                dma((DEG + 1,)), dma((DEG + 1,)), dma((DEG + 1,)), dma((DEG + 1,)),
                dma((5,)), dma((5,)),
                dma((8,)), dma((8,)), dma((n_domain // 8,)), dma((n_domain // 8,)), dma((8,)), dma((8,)),
            ],
            compiler_params=pltpu.CompilerParams(
                collective_id=0, has_side_effects=True, vmem_limit_bytes=60 * 2**20
            ),
        )(
            orbitals,
            potential.reshape(nodes // LOC, LOC),
            cell_scale.reshape(1, cells),
            connectivity.T,
            boundary.reshape(ghosts // LOC, LOC),
            jnp.asarray(tile),
        )
        return pl.pallas_call(
            write_out,
            name="outputs",
            out_shape=(
                jax.ShapeDtypeStruct((states, nodes), F32),
                jax.ShapeDtypeStruct((states, everyone), F32),
                jax.ShapeDtypeStruct((states, everyone), F32),
            ),
            in_specs=[pl.BlockSpec(memory_space=vm)] * 2,
            out_specs=(pl.BlockSpec(memory_space=vm),) * 3,
        )(filtered, totals)

    in_specs = (P("band", "domain"), P("domain"), P("domain"), P(None, "domain"), P("domain"))
    out_specs = (P("band", "domain"), P("band", None), P("band", None))
    return jax.shard_map(
        per_device, mesh=mesh, in_specs=in_specs, out_specs=out_specs, check_vma=False
    )
```

```python
import math

import jax
import jax.numpy as jnp
import numpy as np
from jax import lax
from jax.experimental import pallas as pl
from jax.experimental.pallas import tpu as pltpu
from jax.sharding import PartitionSpec as P

DEG = 4
CENTRE = 5.0
SPREAD = 4.0
MESH = pl.DeviceIdType.MESH
F32 = jnp.float32
BF16 = jnp.bfloat16
F8 = jnp.float8_e4m3fn
PIECES = 4
PRODUCT_PIECES = 3
STEP = 32.0
TOP = 128.0
LOC = 128
CHUNK = 512
PART = 8


def gauss_rule():
    inner = math.sqrt(5.0 - 2.0 * math.sqrt(10.0 / 7.0)) / 3.0
    outer = math.sqrt(5.0 + 2.0 * math.sqrt(10.0 / 7.0)) / 3.0
    w_inner = (322.0 + 13.0 * math.sqrt(70.0)) / 900.0
    w_outer = (322.0 - 13.0 * math.sqrt(70.0)) / 900.0
    points = np.array([-outer, -inner, 0.0, inner, outer])
    weights = np.array([w_outer, w_inner, 128.0 / 225.0, w_inner, w_outer])
    return (points, weights)


def element_matrix():
    nodes_1d = np.linspace(0.0, 1.0, 5)
    points, weights = gauss_rule()
    points = 0.5 * (points + 1.0)
    weights = 0.5 * weights
    values = np.ones((5, 5))
    slopes = np.zeros((5, 5))
    for i in range(5):
        for j in range(5):
            if j != i:
                values[i] = values[i] * (points - nodes_1d[j]) / (nodes_1d[i] - nodes_1d[j])
                product_term = np.ones(5) / (nodes_1d[i] - nodes_1d[j])
                for m in range(5):
                    if m != i and m != j:
                        product_term = (
                            product_term * (points - nodes_1d[m]) / (nodes_1d[i] - nodes_1d[m])
                        )
                slopes[i] = slopes[i] + product_term
    mass_1d = values * weights @ values.T
    stiffness = slopes * weights @ slopes.T
    whole = (
        np.kron(np.kron(stiffness, mass_1d), mass_1d)
        + np.kron(np.kron(mass_1d, stiffness), mass_1d)
        + np.kron(np.kron(mass_1d, mass_1d), stiffness)
    )
    return whole / np.max(np.sum(np.abs(whole), axis=1))


def element_tile():
    matrix = np.zeros((LOC, LOC), np.float32)
    matrix[:125, :125] = element_matrix().T.astype(np.float32)
    high = matrix.astype(jnp.bfloat16)
    low = (matrix - high.astype(np.float32)).astype(jnp.bfloat16)
    row = np.concatenate([high, low], axis=1)
    return np.concatenate([row, row], axis=0)


def dot(a, b):
    return jnp.dot(a, b, preferred_element_type=F32)


def row_max(x):
    return jnp.maximum(jnp.max(jnp.abs(x), axis=1, keepdims=True), 1e-30)


def cut(x, count):
    pieces = []
    for p in range(count):
        piece = x.astype(F8)
        pieces.append(piece)
        if p < count - 1:
            x = (x - piece.astype(F32)) * STEP
    return pieces


def joined(d, count):
    states = d.shape[0] // count
    total = d[(count - 1) * states :]
    for p in range(count - 2, -1, -1):
        total = d[p * states : (p + 1) * states] + total * (1.0 / STEP)
    return total


def kernel(
    n_domain, n_band, nodes_total,
    orb_in, pot_in, scl_in, conn_in, bnd_in, kk_in,
    filt_out, total_out,
    gt, gs, gpt, gps, bt, bs, pack, packp,
    cur, old, ay, pv, pb, pg, pr, pw, pwp, wo, xs, xsp, r2,
    bsend, grecv, rsend, rrecv,
    fall, lhs, rhs, part, rsrecv, zbuf, tot, pot, scl, conn, bnd, kk, in_s,
    out_s, pk_ss, pk_rs, b_ss, b_rs, r_ss, r_rs, f_ss, f_rs, s1_ss, s1_rs, s2_ss, s2_rs, s3_ss, s3_rs,
):
    fetches = [
        pltpu.make_async_copy(src, dst, in_s.at[i])
        for i, (src, dst) in enumerate(
            (
                (conn_in, conn), (bnd_in, bnd), (scl_in, scl), (orb_in, cur),
                (orb_in, old), (kk_in, kk), (pot_in, pot),
            )
        )
    ]
    for fetch in fetches:
        fetch.start()
    states, nodes = orb_in.shape
    cells = conn.shape[0]
    ghosts = bnd.shape[0] * bnd.shape[1]
    width = cells * LOC
    me = lax.axis_index("domain")
    mb = lax.axis_index("band")
    nxt = lax.rem(me + 1, n_domain)
    prv = lax.rem(me + n_domain - 1, n_domain)
    near = mb + 1 - 2 * lax.rem(mb, 2)
    far = lax.rem(mb + 2, n_band)
    q = lax.rem(me, 8)
    z = me // 8
    zs = n_domain // 8
    base = z * 8

    barrier = pltpu.get_barrier_semaphore()

    def greet(where):
        pl.semaphore_signal(barrier, inc=1, device_id=where, device_id_type=MESH)

    greet({"domain": nxt})
    greet({"domain": prv})
    greet({"band": near})
    greet({"band": far})
    for r in range(1, 8):
        greet({"domain": base + lax.rem(q + r, 8)})
    for r in range(1, zs):
        greet({"domain": lax.rem(z + r, zs) * 8 + q})
    greeted = 4 + 7 + zs - 1

    def copy(src, dst, ss, rs, where):
        return pltpu.make_async_remote_copy(
            src_ref=src, dst_ref=dst, send_sem=ss, recv_sem=rs, device_id=where, device_id_type=MESH
        )

    for fetch in fetches[:3]:
        fetch.wait()
    pack[0:cells, :] = jnp.full((cells, LOC), -1.0, F32)
    pack[0:cells, 0 : conn.shape[1]] = conn[...].astype(F32)
    eye = lax.broadcasted_iota(jnp.int32, (cells, cells), 0) == lax.broadcasted_iota(
        jnp.int32, (cells, cells), 1
    )
    factors = jnp.sum(jnp.where(eye, scl[...], 0.0), axis=1, keepdims=True) * 0.5
    pack[cells : 2 * cells, :] = jnp.broadcast_to(factors, (cells, LOC))

    down = lax.broadcasted_iota(jnp.int32, (LOC, LOC), 0).astype(F32)
    across = lax.broadcasted_iota(jnp.int32, (LOC, LOC), 1).astype(F32)
    nothing = jnp.zeros((LOC, LOC), F8)

    def one_hot(upright, flat, span, row, first, count):
        block = jnp.floor(row * (1.0 / LOC))
        rest = jnp.broadcast_to(row - block * LOC, (LOC, LOC))
        block = jnp.broadcast_to(block, (LOC, LOC))
        hot_u = jnp.where(rest == down, 1.0, 0.0).astype(F8)
        hot_f = jnp.where(rest.T == across, 1.0, 0.0).astype(F8)
        block_u = block.astype(jnp.int32).astype(jnp.int8)
        block_f = block.T.astype(jnp.int32).astype(jnp.int8)
        for t in range(count // LOC):
            at = slice(t * LOC, (t + 1) * LOC)
            now = jnp.int8(first // LOC + t)
            upright[at, span] = jnp.where(block_u == now, hot_u, nothing)
            flat[span, at] = jnp.where(block_f == now, hot_f, nothing)

    def own_matrices(lo, hi):
        @pl.loop(lo, hi, unroll=4)
        def _(c):
            span = pl.ds(pl.multiple_of(c * LOC, LOC), LOC)
            one_hot(gt, gs, span, pack[pl.ds(c, 1), :], 0, nodes + ghosts)

    for g in range(ghosts // LOC):
        one_hot(bt, bs, slice(g * LOC, (g + 1) * LOC), bnd[g : g + 1, :].astype(F32), 0, nodes)
    own_matrices(0, cells // 2)
    pl.semaphore_wait(barrier, greeted)
    pack_copy = copy(pack, packp, pk_ss, pk_rs, {"domain": nxt})
    pack_copy.start()
    own_matrices(cells // 2, cells)

    for fetch in fetches[3:]:
        fetch.wait()

    def put(dst, at, pieces):
        for p, piece in enumerate(pieces):
            dst[p * states : (p + 1) * states, at] = piece

    def gathered(values, upright, rows, dst, lo, hi):
        for n in range(lo * LOC, hi * LOC, CHUNK):
            u = joined(dot(values[...], upright[rows, n : n + CHUNK]), PIECES)
            for i in range(CHUNK // LOC):
                one = u[:, i * LOC : (i + 1) * LOC]
                high = one.astype(BF16)
                at = slice((n // LOC + i) * states, (n // LOC + i + 1) * states)
                dst[at, 0:LOC] = high
                dst[at, LOC : 2 * LOC] = (one - high.astype(F32)).astype(BF16)

    def cell_products(src, factor_rows, use, lo, hi):
        both = dot(src[lo * states : hi * states, :], kk[...])
        for i in range(hi - lo):
            at = slice(i * states, (i + 1) * states)
            use(
                slice((lo + i) * LOC, (lo + i + 1) * LOC),
                (both[at, 0:LOC] + both[at, LOC:]) * factor_rows[lo + i : lo + i + 1, :],
            )

    def elements(values, upright, rows, dst, factor_rows, use):
        gathered(values, upright, rows, dst, 0, cells)
        for c in range(0, cells, PART):
            cell_products(dst, factor_rows, use, c, c + PART)

    own = pack.at[cells : 2 * cells, :]
    before = packp.at[cells : 2 * cells, :]
    f_near = copy(fall.at[mb], fall.at[mb], f_ss.at[0], f_rs.at[0], {"band": near})
    halves = [slice(0, nodes // 2), slice(nodes // 2, nodes)]
    f_far = [
        copy(fall.at[mb, :, h], fall.at[mb, :, h], f_ss.at[1 + i], f_rs.at[1 + i], {"band": far})
        for i, h in enumerate(halves)
    ]
    f_pass = [
        copy(fall.at[far, :, h], fall.at[far, :, h], f_ss.at[3 + i], f_rs.at[3 + i], {"band": near})
        for i, h in enumerate(halves)
    ]

    def border_copy(k):
        return copy(bsend.at[k], grecv.at[k], b_ss.at[k], b_rs.at[k], {"domain": prv})

    def back_copy(k):
        return copy(rsend.at[k], rrecv.at[k], r_ss.at[k], r_rs.at[k], {"domain": nxt})

    f_out = pltpu.make_async_copy(fall.at[mb], filt_out, out_s)

    @pl.loop(0, DEG + 1)
    def _(k):
        first = (k == 0).astype(F32)
        alpha = (2.0 - first) / SPREAD
        beta = 1.0 - first
        y = cur[...]
        top = row_max(y)
        scale, inverse = top * (1.0 / TOP), TOP / top
        put(pv, slice(0, nodes), cut(y * inverse, PIECES))
        d = dot(pv[...], bt[...])
        pb[...] = d.astype(F8)
        bsend[k] = joined(d, PIECES) * scale
        border_copy(k).start()

        @pl.when(k == DEG)
        def _():
            fall[mb] = cur[...]
            f_near.start()
            f_far[0].start()
            f_out.start()

        def keep(at, w):
            wo[:, at] = w
            put(pw, at, cut(w, PRODUCT_PIECES))

        elements(pv, gt, slice(0, nodes), xs, own, keep)
        rsend[k] = joined(dot(pw[...], gs[:, nodes:]), PRODUCT_PIECES) * scale
        back_copy(k).start()

        @pl.when(k == DEG)
        def _():
            f_far[1].start()

        @pl.when(k == 0)
        def _():
            pack_copy.wait()

            @pl.loop(0, cells, unroll=4)
            def _(c):
                span = pl.ds(pl.multiple_of(c * LOC, LOC), LOC)
                one_hot(gpt, gps, span, packp[pl.ds(c, 1), :], nodes, ghosts)

        elements(
            pb, gpt, slice(0, ghosts), xsp, before,
            lambda at, w: put(pwp, at, cut(w, PRODUCT_PIECES)),
        )
        r2[...] = joined(dot(pwp[...], gps[...]), PRODUCT_PIECES) * scale

        border_copy(k).wait_recv()
        ghost = grecv[k]
        top_g = row_max(ghost)
        put(pg, slice(0, ghosts), cut(ghost * (TOP / top_g), PIECES))
        both = jnp.maximum(top, top_g)
        ratio, ratio_g, scale_b = top / both, top_g / both, both * (1.0 / TOP)
        elements(
            pg, gt, slice(nodes, nodes + ghosts), xs, own,
            lambda at, w: put(pw, at, cut(wo[:, at] * ratio + w * ratio_g, PRODUCT_PIECES)),
        )
        for n in range(0, nodes, CHUNK):
            at = slice(n, n + CHUNK)
            h = joined(dot(pw[...], gs[:, at]), PRODUCT_PIECES) * scale_b
            for i in range(CHUNK // LOC):
                at = slice(n + i * LOC, n + (i + 1) * LOC)
                t = n // LOC + i
                v = cur[:, at]
                full = h[:, i * LOC : (i + 1) * LOC] + pot[t : t + 1, :] * v
                ay[:, at] = full
                cur[:, at] = alpha * (full - CENTRE * v) - beta * old[:, at]
                old[:, at] = v

        @pl.when(k == DEG)
        def _():
            f_far[0].wait_recv()
            f_pass[0].start()

        back_copy(k).wait_recv()
        shared = rrecv[k] + r2[...]
        top_r = row_max(shared)
        put(pr, slice(0, ghosts), cut(shared * (TOP / top_r), PIECES))
        for n in range(0, nodes, CHUNK):
            at = slice(n, n + CHUNK)
            h = joined(dot(pr[...], bs[:, n : n + CHUNK]), PIECES) * (top_r * (1.0 / TOP))
            ay[:, at] = ay[:, at] + h
            cur[:, at] = cur[:, at] + alpha * h

    f_far[1].wait_recv()
    f_pass[1].start()
    for i, value in enumerate((old, ay)):
        v = value[...]
        high = v.astype(BF16)
        lhs[2 * i * states : (2 * i + 1) * states, :] = high
        lhs[(2 * i + 1) * states : (2 * i + 2) * states, :] = (v - high.astype(F32)).astype(BF16)
    f_near.wait_recv()
    f_pass[0].wait_recv()
    f_pass[1].wait_recv()
    everyone = n_band * states
    for j in range(n_band):
        v = fall[j]
        high = v.astype(BF16)
        rhs[j * states : (j + 1) * states, :] = high
        rhs[everyone + j * states : everyone + (j + 1) * states, :] = (v - high.astype(F32)).astype(BF16)
    g = lax.dot_general(
        lhs[...], rhs[...], (((1,), (1,)), ((), ())), preferred_element_type=F32
    )
    g = g[:, :everyone] + g[:, everyone:]
    part[0 : states // 8] = (g[0:states] + g[states : 2 * states]).reshape(states // 8, 8, everyone)
    part[states // 8 :] = (g[2 * states : 3 * states] + g[3 * states :]).reshape(
        states // 8, 8, everyone
    )

    sends, sent = [], []
    for r in range(1, 8):
        peer = lax.rem(q + r, 8)
        c = copy(part.at[peer], rsrecv.at[r], s1_ss.at[r], s1_rs.at[r], {"domain": base + peer})
        c.start()
        sends.append(c)
    for c in sends:
        c.wait_recv()
    sent += sends
    total = part[q]
    for r in range(1, 8):
        total = total + rsrecv[r]
    zbuf[z] = total
    sends = []
    for r in range(1, zs):
        peer = lax.rem(z + r, zs)
        c = copy(zbuf.at[z], zbuf.at[z], s2_ss.at[r], s2_rs.at[r], {"domain": peer * 8 + q})
        c.start()
        sends.append(c)
    for c in sends:
        c.wait_recv()
    sent += sends
    total = zbuf[0]
    for r in range(1, zs):
        total = total + zbuf[r]
    tot[q] = total * (1.0 / nodes_total)
    sends = []
    for r in range(1, 8):
        peer = lax.rem(q + r, 8)
        c = copy(tot.at[q], tot.at[q], s3_ss.at[r], s3_rs.at[r], {"domain": base + peer})
        c.start()
        sends.append(c)
    for c in sends:
        c.wait_recv()
    sent += sends
    total_out[...] = tot[...].reshape(2 * states, everyone)
    for k in range(DEG + 1):
        border_copy(k).wait_send()
        back_copy(k).wait_send()
    for c in sent + [f_near] + f_far + f_pass:
        c.wait_send()
    f_out.wait()


def write_out(filt, total, filt_out, inter_out, proj_out):
    states = filt.shape[0]
    filt_out[...] = filt[...]
    inter_out[...] = total[0:states, :]
    proj_out[...] = total[states:, :]


def solution(mesh):
    n_domain, n_band = mesh.shape["domain"], mesh.shape["band"]
    tile = element_tile()

    def per_device(orbitals, potential, cell_scale, connectivity, boundary):
        states, nodes = orbitals.shape
        cells = connectivity.shape[1]
        ghosts = boundary.shape[0]
        width = cells * LOC
        rows = PIECES * states
        everyone = n_band * states
        vm = pltpu.VMEM
        dma = pltpu.SemaphoreType.DMA
        body = lambda *refs: kernel(n_domain, n_band, nodes * n_domain, *refs)
        filtered, totals = pl.pallas_call(
            body,
            name="chebyshev_step",
            out_shape=(
                jax.ShapeDtypeStruct((states, nodes), F32),
                jax.ShapeDtypeStruct((2 * states, everyone), F32),
            ),
            in_specs=[pl.BlockSpec(memory_space=pl.ANY)] * 6,
            out_specs=(pl.BlockSpec(memory_space=pl.ANY), pl.BlockSpec(memory_space=vm)),
            scratch_shapes=[
                vm((nodes + ghosts, width), F8),
                vm((width, nodes + ghosts), F8),
                vm((ghosts, width), F8),
                vm((width, ghosts), F8),
                vm((nodes, ghosts), F8),
                vm((ghosts, nodes), F8),
                vm((2 * cells, LOC), F32),
                vm((2 * cells, LOC), F32),
                vm((states, nodes), F32),
                vm((states, nodes), F32),
                vm((states, nodes), F32),
                vm((rows, nodes), F8),
                vm((rows, ghosts), F8),
                vm((rows, ghosts), F8),
                vm((rows, ghosts), F8),
                vm((PRODUCT_PIECES * states, width), F8),
                vm((PRODUCT_PIECES * states, width), F8),
                vm((states, width), F32),
                vm((cells * states, 2 * LOC), BF16),
                vm((cells * states, 2 * LOC), BF16),
                vm((states, ghosts), F32),
                vm((DEG + 1, states, ghosts), F32),
                vm((DEG + 1, states, ghosts), F32),
                vm((DEG + 1, states, ghosts), F32),
                vm((DEG + 1, states, ghosts), F32),
                vm((n_band, states, nodes), F32),
                vm((4 * states, nodes), BF16),
                vm((2 * everyone, nodes), BF16),
                vm((8, 8, everyone), F32),
                vm((8, 8, everyone), F32),
                vm((n_domain // 8, 8, everyone), F32),
                vm((8, 8, everyone), F32),
                vm((nodes // LOC, LOC), F32),
                vm((1, cells), F32),
                vm((cells, connectivity.shape[0]), jnp.int32),
                vm((ghosts // LOC, LOC), jnp.int32),
                vm((2 * LOC, 2 * LOC), BF16),
                dma((7,)),
                dma, dma, dma,
                dma((DEG + 1,)), dma((DEG + 1,)), dma((DEG + 1,)), dma((DEG + 1,)),
                dma((5,)), dma((5,)),
                dma((8,)), dma((8,)), dma((n_domain // 8,)), dma((n_domain // 8,)), dma((8,)), dma((8,)),
            ],
            compiler_params=pltpu.CompilerParams(
                collective_id=0, has_side_effects=True, vmem_limit_bytes=60 * 2**20
            ),
        )(
            orbitals,
            potential.reshape(nodes // LOC, LOC),
            cell_scale.reshape(1, cells),
            connectivity.T,
            boundary.reshape(ghosts // LOC, LOC),
            jnp.asarray(tile),
        )
        return pl.pallas_call(
            write_out,
            name="outputs",
            out_shape=(
                jax.ShapeDtypeStruct((states, nodes), F32),
                jax.ShapeDtypeStruct((states, everyone), F32),
                jax.ShapeDtypeStruct((states, everyone), F32),
            ),
            in_specs=[pl.BlockSpec(memory_space=vm)] * 2,
            out_specs=(pl.BlockSpec(memory_space=vm),) * 3,
        )(filtered, totals)

    in_specs = (P("band", "domain"), P("domain"), P("domain"), P(None, "domain"), P("domain"))
    out_specs = (P("band", "domain"), P("band", None), P("band", None))
    return jax.shard_map(
        per_device, mesh=mesh, in_specs=in_specs, out_specs=out_specs, check_vma=False
    )
```
